32 devices in a mesh: section: 4 (over y, x), dp: 8 (over z, core).
Axes of the slice: x: 2, y: 2, z: 4, core: 2. Of those that a mesh axis runs over, the one named last changes fastest.
Arguments:
- tokens: bfloat16 [3840, 2048], P('dp'), may hold values from -6 to 6
- cotangent: bfloat16 [3840, 2048], P('dp'), may hold values from -6 to 6
- w_gate: bfloat16 [4, 2048, 512], P('section'), may hold values from -0.125 to 0.125
- w_up: bfloat16 [4, 2048, 512], P('section'), may hold values from -0.125 to 0.125
- w_down: bfloat16 [4, 2048, 512], P('section'), may hold values from -0.25 to 0.25
Outputs:
- input_grad: bfloat16 [4, 3840, 2048], P('section', 'dp')
- grad_gate: float32 [4, 2048, 512], P('section', 'dp')
- grad_up: float32 [4, 2048, 512], P('section', 'dp')
- grad_down: float32 [4, 2048, 512], P('section', 'dp')
The draws below stay inside these ranges and needn't reach their ends.
All inputs are finite; a program needn't handle non-finite values.
Results may differ from the reference program's by a relative error of at most 0.035.
Values may be sent and summed in bfloat16 or wider, within the bound.
No kernel may reach another device: no remote copies, remote signals or barrier semaphores. Data moves between devices by JAX's collectives and lax.ppermute only.
A program may use at most 128 MiB of HBM per device.

```python
import jax
import jax.numpy as jnp
from jax import lax

D = 2048
F = 512
TOKENS = 3840
LAYERS = 4


def spiked(result, stream_key, source, target, blocks, factor):
    def block_of(axis_at):
        return (jnp.arange(result.shape[axis_at]) // (result.shape[axis_at] // blocks)).reshape((-1,) + (1,) * (result.ndim - 1 - axis_at))

    one_side = jax.random.permutation(stream_key, blocks)[block_of(target)]
    far = (block_of(target) + blocks // 2) % blocks
    return jnp.where((block_of(source) == one_side) | (block_of(source) == far), factor * result, result)


def level_of(stream_key, shape, shards, smallest, largest):
    level, own = 1.0, jax.random.fold_in(stream_key, 6)
    for dim, blocks in shards:
        heights = jnp.exp(jax.random.uniform(jax.random.fold_in(own, dim), (blocks,), jnp.float32, smallest / len(shards), largest / len(shards)))
        level = level * jnp.repeat(heights, shape[dim] // blocks).reshape([-1 if axis == dim else 1 for axis in range(len(shape))])
    return level


def normal_values(stream_key, shape, width, bound, shards=(), kind=jnp.bfloat16):
    values = jax.random.normal(stream_key, shape, jnp.float32) * width
    if len(shards) > 0:
        values = level_of(stream_key, shape, shards, -0.22, 0.18) * values
    return jnp.clip(values, min=-bound, max=bound).astype(kind)


def heavy_noise(own_key, shape, width, reach, pieces, heavy, kind=jnp.bfloat16):
    values = width * jax.random.normal(own_key, shape, jnp.float32)
    if pieces:
        values = values * level_of(own_key, shape, pieces, -0.22, 0.18)
    return jnp.clip(spiked(values, jax.random.fold_in(own_key, 3), *heavy), -reach, reach).astype(kind)


def setup_inputs(seed: int = 0) -> dict:
    streams_of = jax.random.split(jax.random.key(seed), 6)
    return {
        "tokens": heavy_noise(streams_of[0], (TOKENS, D), 1.0, 6.0, ((0, 8),), (0, 1, 8, 2.0)),
        "cotangent": heavy_noise(streams_of[1], (TOKENS, D), 1.0, 6.0, ((0, 8),), (0, 1, 8, 2.0)),
        "w_gate": normal_values(streams_of[2], (LAYERS, D, F), D ** -0.5, 0.125, ((0, 4),)),
        "w_up": normal_values(streams_of[3], (LAYERS, D, F), D ** -0.5, 0.125, ((0, 4),)),
        "w_down": normal_values(streams_of[4], (LAYERS, D, F), F ** -0.5, 0.25, ((0, 4),)),
    }


def forward_layer(layer_input_rows, w_gate, w_up, w_down):
    xf = layer_input_rows.astype(jnp.float32)
    inverse_norm_scale = lax.rsqrt(lax.optimization_barrier(jnp.mean(xf * xf, axis=-1, keepdims=True)) + 1e-06)
    normed = (xf * inverse_norm_scale).astype(jnp.bfloat16)
    gate = jnp.dot(normed, w_gate, preferred_element_type=jnp.float32)
    upper = jnp.dot(normed, w_up, preferred_element_type=jnp.float32)
    hidden = (gate * jax.nn.sigmoid(gate) * upper).astype(jnp.bfloat16)
    branch = lax.dot_general(hidden, w_down, (((1,), (1,)), ((), ())), preferred_element_type=jnp.float32)
    return ((xf + branch).astype(jnp.bfloat16), normed, inverse_norm_scale, gate, upper, hidden)

def backward_layer(layer_input_rows, arriving_gradient, inverse_norm_scale, gate, upper, w_gate, w_up, w_down):
    d_hidden = jnp.dot(arriving_gradient, w_down, preferred_element_type=jnp.float32)
    sig = jax.nn.sigmoid(gate)
    d_gate = (d_hidden * upper * sig * (1.0 + gate * (1.0 - sig))).astype(jnp.bfloat16)
    d_upper = (d_hidden * gate * sig).astype(jnp.bfloat16)
    dims = (((1,), (1,)), ((), ()))
    normalized_gradient = lax.dot_general(d_gate, w_gate, dims, preferred_element_type=jnp.float32)
    normalized_gradient = normalized_gradient + lax.dot_general(d_upper, w_up, dims, preferred_element_type=jnp.float32)
    normalized_input = layer_input_rows.astype(jnp.float32) * inverse_norm_scale
    inner_product_sum = lax.optimization_barrier(jnp.mean(normalized_gradient * normalized_input, axis=-1, keepdims=True))
    input_gradient_rows = (arriving_gradient.astype(jnp.float32) + inverse_norm_scale * (normalized_gradient - normalized_input * inner_product_sum)).astype(jnp.bfloat16)
    return (input_gradient_rows, d_gate, d_upper)

def reference(tokens, cotangent, w_gate, w_up, w_down):
    rows_dims = (((0,), (0,)), ((), ()))
    current = tokens
    inputs = []
    for layer in range(LAYERS):
        inputs.append(current)
        current = forward_layer(current, w_gate[layer], w_up[layer], w_down[layer])[0]
    arriving_gradient = cotangent
    grads_in = [None] * LAYERS
    grads_g = [None] * LAYERS
    grads_u = [None] * LAYERS
    grads_d = [None] * LAYERS
    for layer in reversed(range(LAYERS)):
        layer_input_rows = inputs[layer]
        _, normed, inverse_norm_scale, gate, upper, hidden = forward_layer(layer_input_rows, w_gate[layer], w_up[layer], w_down[layer])
        input_gradient_rows, d_gate, d_upper = backward_layer(layer_input_rows, arriving_gradient, inverse_norm_scale, gate, upper, w_gate[layer], w_up[layer], w_down[layer])
        grads_g[layer] = lax.dot_general(normed, d_gate, rows_dims, preferred_element_type=jnp.float32)
        grads_u[layer] = lax.dot_general(normed, d_upper, rows_dims, preferred_element_type=jnp.float32)
        grads_d[layer] = lax.dot_general(arriving_gradient, hidden, rows_dims, preferred_element_type=jnp.float32)
        grads_in[layer] = input_gradient_rows
        arriving_gradient = input_gradient_rows
    return (jnp.stack(grads_in), jnp.stack(grads_g), jnp.stack(grads_u), jnp.stack(grads_d))
```

```python
import functools

import jax
import jax.numpy as jnp
from jax import lax
from jax.experimental import pallas as pl
from jax.experimental.pallas import tpu as pltpu
from jax.sharding import PartitionSpec as P

ROWS = 64
LAG_F = 2
LAG_B = 2


f32 = jnp.float32
bf16 = jnp.bfloat16
NT = (((1,), (1,)), ((), ()))
TN = (((0,), (0,)), ((), ()))
VM = pl.BlockSpec(memory_space=pltpu.VMEM)
SM = pl.BlockSpec(memory_space=pltpu.SMEM)


def shape_of(*dims, dtype=bf16):
    return jax.ShapeDtypeStruct(dims, dtype)


def params():
    return pltpu.CompilerParams(vmem_limit_bytes=12 << 20)


def starts_of(total, rows):
    return [min(i * rows, total - rows) for i in range(-(-total // rows))]


def forward_kernel(tick, micro, rows, has_arrived, *refs):
    refs = list(refs)
    place, last = refs.pop(0)[0], refs.pop(0)[0]
    tokens, w_gate, w_up, w_down = refs[:4]
    out, saved_gate, saved_up, source = refs[-4:]
    index = tick - LAG_F * place
    total = tokens.shape[0]

    @pl.when((index >= 0) & (index < micro))
    def work():
        def own():
            start = pl.multiple_of(jnp.minimum(index * rows, total - rows), 16)
            source[...] = tokens[pl.ds(start, rows), :]

        if has_arrived:
            pl.when(place == 0)(own)

            @pl.when(place != 0)
            def passed():
                source[...] = refs[4][...]

        else:
            own()
        xf = source[...].astype(f32)
        scale = lax.rsqrt(jnp.mean(xf * xf, axis=-1, keepdims=True) + 1e-06)
        normed = (xf * scale).astype(bf16)
        gate = jnp.dot(normed, w_gate[...], preferred_element_type=f32)
        upper = jnp.dot(normed, w_up[...], preferred_element_type=f32)
        saved_gate[...] = gate
        saved_up[...] = upper

        @pl.when(place != last)
        def down():
            hidden = (gate * jax.nn.sigmoid(gate) * upper).astype(bf16)
            branch = lax.dot_general(hidden, w_down[...], NT, preferred_element_type=f32)
            out[...] = (source[...].astype(f32) + branch).astype(bf16)


def forward_call(tick, micro, rows, place, last, tokens, weights, arrived):
    width = tokens.shape[1]
    units = weights[0].shape[1]
    operands = [place, last, tokens, *weights]
    if arrived is not None:
        operands.append(arrived)
    return pl.pallas_call(
        functools.partial(forward_kernel, tick, micro, rows, arrived is not None),
        out_shape=[
            shape_of(rows, width),
            shape_of(rows, units, dtype=f32),
            shape_of(rows, units, dtype=f32),
        ],
        in_specs=[SM, SM] + [VM] * (len(operands) - 2),
        out_specs=[VM] * 3,
        scratch_shapes=[pltpu.VMEM((rows, width), bf16)],
        compiler_params=params(),
        cost_estimate=pl.CostEstimate(
            flops=6 * rows * width * units, bytes_accessed=6 * width * units, transcendentals=0
        ),
        name="forward",
    )(*operands)


def backward_kernel(back, micro, rows, places, has_arrived, *refs):
    refs = list(refs)
    place, last = refs.pop(0)[0], refs.pop(0)[0]
    tokens, cotangent, w_gate, w_up, w_down = refs[:5]
    refs = refs[5:]
    arrived = refs.pop(0) if has_arrived else None
    saved = []
    for at in places:
        count = 2 if at == 0 else 3
        saved.append((at, refs[:count]))
        refs = refs[count:]
    out, norms, d_gates, d_ups, hiddens, source, gates, ups, grads = refs
    index = back - LAG_B * (last - place)
    total = cotangent.shape[0]
    start = pl.multiple_of(jnp.clip(index * rows, 0, total - rows), 16)

    @pl.when((index >= 0) & (index < micro))
    def work():
        for at, kept in saved:

            @pl.when(place == at)
            def take():
                gates[...] = kept[0][...]
                ups[...] = kept[1][...]
                source[...] = tokens[pl.ds(start, rows), :] if at == 0 else kept[2][...]

        def own():
            grads[...] = cotangent[pl.ds(start, rows), :]

        if has_arrived:
            pl.when(place == last)(own)

            @pl.when(place != last)
            def passed():
                grads[...] = arrived[...]

        else:
            own()
        grad_in = grads[...]
        gate = gates[...]
        upper = ups[...]
        d_hidden = jnp.dot(grad_in, w_down[...], preferred_element_type=f32)
        sig = jax.nn.sigmoid(gate)
        d_gate = (d_hidden * upper * sig * (1.0 + gate * (1.0 - sig))).astype(bf16)
        d_up = (d_hidden * gate * sig).astype(bf16)
        d_gates[...] = d_gate
        d_ups[...] = d_up
        hiddens[...] = (gate * sig * upper).astype(bf16)
        d_norm = lax.dot_general(d_gate, w_gate[...], NT, preferred_element_type=f32)
        d_norm = d_norm + lax.dot_general(d_up, w_up[...], NT, preferred_element_type=f32)
        xf = source[...].astype(f32)
        scale = lax.rsqrt(jnp.mean(xf * xf, axis=-1, keepdims=True) + 1e-06)
        x_hat = xf * scale
        norms[...] = x_hat.astype(bf16)
        inner = jnp.mean(d_norm * x_hat, axis=-1, keepdims=True)
        out[...] = (grad_in.astype(f32) + scale * (d_norm - x_hat * inner)).astype(bf16)


def backward_call(back, micro, rows, place, last, tokens, cotangent, weights, arrived, saved):
    width = cotangent.shape[1]
    units = weights[0].shape[1]
    operands = [place, last, tokens, cotangent, *weights]
    if arrived is not None:
        operands.append(arrived)
    for _, kept in saved:
        operands += kept
    return pl.pallas_call(
        functools.partial(
            backward_kernel, back, micro, rows, [at for at, _ in saved], arrived is not None
        ),
        out_shape=[
            shape_of(rows, width),
            shape_of(rows, width),
            shape_of(rows, units),
            shape_of(rows, units),
            shape_of(rows, units),
        ],
        in_specs=[SM, SM] + [VM] * (len(operands) - 2),
        out_specs=[VM] * 5,
        scratch_shapes=[
            pltpu.VMEM((rows, width), bf16),
            pltpu.VMEM((rows, units), f32),
            pltpu.VMEM((rows, units), f32),
            pltpu.VMEM((rows, width), bf16),
        ],
        compiler_params=params(),
        cost_estimate=pl.CostEstimate(
            flops=6 * rows * width * units, bytes_accessed=6 * width * units, transcendentals=0
        ),
        name="backward",
    )(*operands)


def collect_call(micro, rows, sections, place, total, whole, sources):
    width = sources[-1].shape[1]
    has_whole = whole is not None
    lag = 0 if not has_whole else LAG_B

    def kernel(place_ref, *refs):
        refs = list(refs)
        full = refs.pop(0) if has_whole else None
        target = refs.pop()
        pad = [None] * lag + refs
        for at in range(sections):

            @pl.when(place_ref[0] == at)
            def take():
                if has_whole and at == sections - 1:
                    target[...] = full[...]
                else:
                    for i, start in enumerate(starts_of(total, rows)):
                        target[start : start + rows, :] = pad[i + LAG_B * (sections - 1 - at)][...]

    operands = [place] + ([whole] if has_whole else []) + sources[lag:]
    return pl.pallas_call(
        kernel,
        out_shape=shape_of(total, width),
        in_specs=[SM] + [VM] * (len(operands) - 1),
        out_specs=VM,
        compiler_params=params(),
        cost_estimate=pl.CostEstimate(flops=0, bytes_accessed=4 * total * width, transcendentals=0),
        name="collect",
    )(*operands)


def weight_kernel(chips, core_ref, left, right, keep, send):
    core = core_ref[0]
    pair = left.shape[1] // chips
    half = pair // 2
    for chip in range(chips):
        columns = left[:, chip * pair : (chip + 1) * pair]
        both = lax.dot_general(columns, right[...], TN, preferred_element_type=f32)
        both = both.astype(bf16)
        low, high = both[:half], both[half:]

        @pl.when(core == 0)
        def even():
            keep[chip] = low
            send[chip] = high

        @pl.when(core != 0)
        def odd():
            keep[chip] = high
            send[chip] = low


def weight_call(chips, core, left, right):
    total, width = left.shape
    units = right.shape[1]
    half = width // chips // 2
    return pl.pallas_call(
        functools.partial(weight_kernel, chips),
        out_shape=[shape_of(chips, half, units)] * 2,
        in_specs=[SM, VM, VM],
        out_specs=[VM, VM],
        compiler_params=params(),
        cost_estimate=pl.CostEstimate(
            flops=2 * total * width * units, bytes_accessed=4 * width * units, transcendentals=0
        ),
        name="weight",
    )(core, left, right)


def step_kernel(step, chips, has_arrived, *refs):
    chip = refs[0][0]
    keep, swapped = refs[1:3]
    if has_arrived:
        from_left, from_right = refs[3:5]
    to_right, to_left = refs[-2:]

    @pl.when(chip <= step - 1)
    def rightward():
        block = chips - step + chip
        value = keep[block].astype(f32) + swapped[block].astype(f32)
        if has_arrived:
            value = value + jnp.where(chip > 0, from_left[...].astype(f32), 0.0)
        to_right[...] = value.astype(bf16)

    @pl.when(chip >= chips - step)
    def leftward():
        block = step - chips + chip
        value = keep[block].astype(f32) + swapped[block].astype(f32)
        if has_arrived:
            value = value + jnp.where(chip < chips - 1, from_right[...].astype(f32), 0.0)
        to_left[...] = value.astype(bf16)


def step_call(step, chips, chip, keep, swapped, arrived):
    half, units = keep.shape[1:]
    operands = [chip, keep, swapped] + list(arrived or ())
    return pl.pallas_call(
        functools.partial(step_kernel, step, chips, arrived is not None),
        out_shape=[shape_of(half, units)] * 2,
        in_specs=[SM] + [VM] * (len(operands) - 1),
        out_specs=[VM, VM],
        compiler_params=params(),
        cost_estimate=pl.CostEstimate(flops=half * units, bytes_accessed=half * units, transcendentals=0),
        name="step",
    )(*operands)


def final_kernel(chips, chip_ref, keep, swapped, from_left, from_right, out):
    chip = chip_ref[0]
    value = keep[chip].astype(f32) + swapped[chip].astype(f32)
    value = value + jnp.where(chip > 0, from_left[...].astype(f32), 0.0)
    value = value + jnp.where(chip < chips - 1, from_right[...].astype(f32), 0.0)
    out[...] = value


def final_call(chips, chip, keep, swapped, from_left, from_right):
    half, units = keep.shape[1:]
    return pl.pallas_call(
        functools.partial(final_kernel, chips),
        out_shape=shape_of(half, units, dtype=f32),
        in_specs=[SM] + [VM] * 4,
        out_specs=VM,
        compiler_params=params(),
        cost_estimate=pl.CostEstimate(flops=half * units, bytes_accessed=half * units, transcendentals=0),
        name="final",
    )(chip, keep, swapped, from_left, from_right)


def body(tokens, cotangent, w_gate, w_up, w_down):
    sections = lax.axis_size("section")
    lanes = lax.axis_size("dp")
    chips = lanes // 2
    total, width = tokens.shape
    rows = ROWS
    micro = -(-total // rows)
    last_place = sections - 1
    place = lax.axis_index("section").astype(jnp.int32)[None]
    lane = lax.axis_index("dp").astype(jnp.int32)
    core = (lane % 2)[None]
    chip = (lane // 2)[None]
    last = jnp.full((1,), last_place, jnp.int32)
    weights = (w_gate[0], w_up[0], w_down[0])

    begin = LAG_F * last_place
    ticks = micro + begin + LAG_B * last_place
    sent_f, sent_b, kept = {}, {}, {}
    outs = []
    arrivals = []
    for tick in range(ticks):
        if any(0 <= tick - LAG_F * s < micro for s in range(sections)):
            arrived = sent_f.pop(tick - LAG_F, None)
            out, gate, upper = forward_call(
                tick, micro, rows, place, last, tokens, weights, arrived
            )
            kept[tick] = (gate, upper, arrived)
            route = [(s, s + 1) for s in range(last_place) if 0 <= tick - LAG_F * s < micro]
            if route:
                sent_f[tick] = lax.ppermute(out, "section", route)
        back = tick - begin
        if back >= 0:
            arrived = sent_b.pop(tick - LAG_B, None)
            arrivals.append(arrived)
            saved = []
            for s in range(sections):
                index = back - LAG_B * (last_place - s)
                if 0 <= index < micro:
                    entry = kept[index + LAG_F * s]
                    saved.append((s, entry[: 2 if s == 0 else 3]))
            out, *terms = backward_call(
                back, micro, rows, place, last, tokens, cotangent, weights, arrived, saved
            )
            outs.append([out] + terms)
            route = [
                (s, s - 1)
                for s in range(1, sections)
                if 0 <= back - LAG_B * (last_place - s) < micro
            ]
            if route:
                sent_b[tick] = lax.ppermute(out, "section", route)

    laid = functools.partial(collect_call, micro, rows, sections, place, total)
    all_in = laid(cotangent, arrivals)
    all_grad, normed, d_gates, d_ups, hiddens = [laid(None, list(term)) for term in zip(*outs)]
    swap = [(i, i ^ 1) for i in range(lanes)]
    results = []
    for left, right in ((all_in, hiddens), (normed, d_ups), (normed, d_gates)):
        keep, send = weight_call(chips, core, left, right)
        swapped = lax.ppermute(send, "dp", swap)
        arrived = None
        for step in range(1, chips):
            to_right, to_left = step_call(step, chips, chip, keep, swapped, arrived)
            right_route = [
                (2 * z + c, 2 * z + 2 + c) for z in range(min(step, chips - 1)) for c in range(2)
            ]
            left_route = [
                (2 * z + c, 2 * z - 2 + c)
                for z in range(max(chips - step, 1), chips)
                for c in range(2)
            ]
            arrived = (
                lax.ppermute(to_right, "dp", right_route),
                lax.ppermute(to_left, "dp", left_route),
            )
        results.append(final_call(chips, chip, keep, swapped, *arrived))
    grad_d, grad_u, grad_g = results
    return (all_grad[None], grad_g[None], grad_u[None], grad_d[None])


def solution(mesh):
    placed = (
        P("dp", None),
        P("dp", None),
        P("section", None, None),
        P("section", None, None),
        P("section", None, None),
    )
    return jax.shard_map(
        body,
        mesh=mesh,
        in_specs=placed,
        out_specs=(
            P("section", "dp", None),
            P("section", "dp", None),
            P("section", "dp", None),
            P("section", "dp", None),
        ),
        check_vma=False,
    )
```

```python
import functools

import jax
import jax.numpy as jnp
from jax import lax
from jax.experimental import pallas as pl
from jax.experimental.pallas import tpu as pltpu
from jax.sharding import PartitionSpec as P

ROWS = 64
LAG = 2
PIECES_F = 2
PIECES_B = 2


f32 = jnp.float32
bf16 = jnp.bfloat16
NT = (((1,), (1,)), ((), ()))
TN = (((0,), (0,)), ((), ()))
VM = pl.BlockSpec(memory_space=pltpu.VMEM)


def shape_of(*dims, dtype=bf16):
    return jax.ShapeDtypeStruct(dims, dtype)


def pieces(size, count, body):
    step = size // count
    if count == 1:
        body(pl.ds(0, size))
        return

    def one(i, carry):
        body(pl.ds(pl.multiple_of(i * step, step), step))
        return carry

    lax.fori_loop(0, count, one, 0)


def place_of(start, size):
    return pl.ds(start if isinstance(start, int) else pl.multiple_of(start, size), size)


def tick_kernel(tick, micro, rows, sections, plan, *refs):
    runs_f, runs_b, routes, arrivals, places, inputs = plan
    refs = list(refs)
    place = lax.axis_index("section")
    tokens = refs.pop(0) if inputs[0] else None
    cotangent = refs.pop(0) if inputs[1] else None
    w_gate, w_up, w_down = refs[:3]
    refs = refs[3:]
    arrived = [(refs.pop(0), takers) for takers in arrivals]
    saved = []
    for at in places:
        count = 2 if at == 0 else 3
        saved.append((at, refs[:count]))
        refs = refs[count:]
    outs = [refs.pop(0) for _ in routes]
    if runs_f:
        gate_f, up_f = refs[:2]
        refs = refs[2:]
    if runs_b:
        new_grad, norms, terms = refs[:3]
        refs = refs[3:]
    x_f, x_b, gate_b, up_b, grad_in, normed, hidden, wide = refs
    last = sections - 1
    units = w_gate.shape[1]
    index_f = tick - LAG * place
    index_b = tick - LAG * last - LAG * (last - place)

    def window(index, source):
        total = source.shape[0]
        start = jnp.clip(index * rows, 0, total - rows)
        return source[pl.ds(pl.multiple_of(start, 16), rows), :]

    good_f = (index_f >= 0) & (index_f < micro)
    good_b = (index_b >= 0) & (index_b < micro)

    def emit(kind, columns, value):
        for out, route in zip(outs, routes):
            senders = [s for s, what in route if what == kind]
            if senders:
                hit = functools.reduce(jnp.logical_or, [place == s for s in senders])

                @pl.when(hit)
                def send():
                    out[:, columns] = value

    def receive(kind, target, source, owner, index):
        if source is not None:

            @pl.when(place == owner)
            def own():
                target[...] = window(index, source)

        for value, takers in arrived:
            for s, what in takers:
                if what == kind:

                    @pl.when(place == s)
                    def passed():
                        target[...] = value[...]

    if runs_f:

        @pl.when(good_f)
        def forward():
            receive("f", x_f, tokens, 0, index_f)
            xf = x_f[...].astype(f32)
            scale = lax.rsqrt(jnp.mean(xf * xf, axis=-1, keepdims=True) + 1e-06)
            normed[...] = (xf * scale).astype(bf16)

            def entry(columns):
                value = normed[...]
                gate = jnp.dot(value, w_gate[:, columns], preferred_element_type=f32)
                upper = jnp.dot(value, w_up[:, columns], preferred_element_type=f32)
                gate_f[:, columns] = gate
                up_f[:, columns] = upper
                hidden[:, columns] = (gate * jax.nn.sigmoid(gate) * upper).astype(bf16)

            pieces(units, PIECES_F, entry)

            @pl.when(place != last)
            def exit_():
                def down(columns):
                    branch = lax.dot_general(
                        hidden[...], w_down[columns, :], NT, preferred_element_type=f32
                    )
                    value = (x_f[:, columns].astype(f32) + branch).astype(bf16)
                    emit("f", columns, value)

                pieces(x_f.shape[1], PIECES_F, down)

    if runs_b:

        @pl.when(good_b)
        def backward():
            receive("b", grad_in, cotangent, last, index_b)
            for at, kept in saved:

                @pl.when(place == at)
                def take():
                    gate_b[...] = kept[0][...]
                    up_b[...] = kept[1][...]
                    x_b[...] = window(index_b, tokens) if at == 0 else kept[2][...]

            if runs_f:

                @pl.when(place == last)
                def same():
                    gate_b[...] = gate_f[...]
                    up_b[...] = up_f[...]
                    x_b[...] = x_f[...]

            def entry(columns):
                d_hidden = jnp.dot(grad_in[...], w_down[:, columns], preferred_element_type=f32)
                gate = gate_b[:, columns]
                upper = up_b[:, columns]
                sig = jax.nn.sigmoid(gate)
                first = columns.start
                size = columns.size
                terms[:, columns] = (gate * sig * upper).astype(bf16)
                d_up = (d_hidden * gate * sig).astype(bf16)
                d_gate = (d_hidden * upper * sig * (1.0 + gate * (1.0 - sig))).astype(bf16)
                terms[:, place_of(units + first, size)] = d_up
                terms[:, place_of(2 * units + first, size)] = d_gate

            pieces(units, PIECES_B, entry)

            def exit_(columns):
                d_norm = lax.dot_general(
                    terms[:, pl.ds(2 * units, units)], w_gate[columns, :], NT, preferred_element_type=f32
                )
                d_norm = d_norm + lax.dot_general(
                    terms[:, pl.ds(units, units)], w_up[columns, :], NT, preferred_element_type=f32
                )
                wide[:, columns] = d_norm

            pieces(x_b.shape[1], PIECES_B, exit_)
            xf = x_b[...].astype(f32)
            scale = lax.rsqrt(jnp.mean(xf * xf, axis=-1, keepdims=True) + 1e-06)
            x_hat = xf * scale
            norms[...] = x_hat.astype(bf16)
            d_norm = wide[...]
            inner = jnp.mean(d_norm * x_hat, axis=-1, keepdims=True)
            grad = grad_in[...].astype(f32) + scale * (d_norm - x_hat * inner)
            grad = grad.astype(bf16)
            new_grad[...] = grad
            emit("b", pl.ds(0, x_b.shape[1]), grad)


def tick_call(tick, micro, rows, sections, arrays, routes, came, saved):
    total, width = arrays[0].shape
    units = arrays[2].shape[1]
    last = sections - 1
    runs_f = 0 <= tick < micro + LAG * last
    runs_b = 0 <= tick - LAG * last < micro + LAG * last
    own_f = 0 <= tick < micro
    own_b = 0 <= tick - LAG * last < micro
    places = [at for at, _ in saved]
    inputs = (own_f or 0 in places, own_b)
    operands = [a for a, used in zip(arrays, inputs) if used] + list(arrays[2:])
    operands += [value for value, _ in came]
    for _, kept in saved:
        operands += kept
    out_shape = [shape_of(rows, width)] * len(routes)
    if runs_f:
        out_shape += [shape_of(rows, units, dtype=f32)] * 2
    if runs_b:
        out_shape += [shape_of(rows, width), shape_of(rows, width), shape_of(rows, 3 * units)]
    plan = (
        runs_f,
        runs_b,
        routes,
        [[(s + 1 if what == "f" else s - 1, what) for s, what in route] for _, route in came],
        places,
        inputs,
    )
    result = pl.pallas_call(
        functools.partial(tick_kernel, tick, micro, rows, sections, plan),
        out_shape=out_shape,
        in_specs=[VM] * len(operands),
        out_specs=[VM] * len(out_shape),
        scratch_shapes=[
            pltpu.VMEM((rows, width), bf16),
            pltpu.VMEM((rows, width), bf16),
            pltpu.VMEM((rows, units), f32),
            pltpu.VMEM((rows, units), f32),
            pltpu.VMEM((rows, width), bf16),
            pltpu.VMEM((rows, width), bf16),
            pltpu.VMEM((rows, units), bf16),
            pltpu.VMEM((rows, width), f32),
        ],
        compiler_params=pltpu.CompilerParams(vmem_limit_bytes=10 << 20),
        cost_estimate=pl.CostEstimate(
            flops=6 * (runs_f + runs_b) * rows * width * units,
            bytes_accessed=6 * width * units,
            transcendentals=0,
        ),
        name="tick",
    )(*operands)
    result = list(result)
    outs = result[: len(routes)]
    rest = result[len(routes) :]
    kept = rest[:2] if runs_f else None
    terms = rest[-3:] if runs_b else None
    return outs, kept, terms


def collect_call(micro, rows, sections, total, whole, sources):
    last = sections - 1
    starts = [min(i * rows, total - rows) for i in range(micro)]
    whole = [] if whole is None else [whole]
    found = []
    at_of = {}
    for tick, value in enumerate(sources):
        by_place = value if isinstance(value, dict) else dict.fromkeys(range(sections), value)
        for at, array in by_place.items():
            known = [i for i, old in enumerate(found) if old is array]
            if not known:
                known = [len(found)]
                found.append(array)
            at_of[tick, at] = known[0]

    def kernel(*refs):
        place = lax.axis_index("section")
        target = refs[-1]
        pool = refs[len(whole) : -1]
        for at in range(sections):

            @pl.when(place == at)
            def take():
                if whole and at == last:
                    target[...] = refs[0][...]
                else:
                    for i, start in enumerate(starts):
                        target[start : start + rows, :] = pool[at_of[i + LAG * (last - at), at]][...]

    operands = whole + found
    width = operands[-1].shape[1]
    return pl.pallas_call(
        kernel,
        out_shape=shape_of(total, width),
        in_specs=[VM] * len(operands),
        out_specs=VM,
        compiler_params=pltpu.CompilerParams(vmem_limit_bytes=10 << 20),
        cost_estimate=pl.CostEstimate(flops=0, bytes_accessed=4 * total * width, transcendentals=0),
        name="collect",
    )(*operands)


def plan_routes(tick, micro, sections):
    last = sections - 1
    sends_f = [s for s in range(last) if 0 <= tick - LAG * s < micro]
    back = tick - LAG * last
    sends_b = [s for s in range(1, sections) if 0 <= back - LAG * (last - s) < micro]
    edges = {(s, s + 1): "f" for s in sends_f}
    edges.update({(s, s - 1): "b" for s in sends_b})
    plans = []

    def take(pairs):
        plans.append({pair: edges.pop(pair) for pair in pairs})

    both = [(s, s + 1) for s in range(last) if (s, s + 1) in edges and (s + 1, s) in edges]
    for parity in (0, 1):
        chosen = [pair for pair in both if pair[0] % 2 == parity]
        if chosen:
            take([p for a, b in chosen for p in ((a, b), (b, a))])
    for kind in ("f", "b"):
        chosen = [pair for pair, what in edges.items() if what == kind]
        if chosen:
            take(chosen)
    routes = []
    for plan in plans:
        full = {a: b for a, b in plan}
        targets = set(full.values())
        for a in sorted(full):
            if a not in targets:
                end = a
                while end in full:
                    end = full[end]
                full[end] = a
        routes.append((full, [(a, what) for (a, _), what in plan.items()]))
    return routes


def permute(value, full, sections, lanes):
    pairs = []
    for s in range(sections):
        for d in range(lanes):
            to = full[s] * lanes + d if s in full else s * lanes + (d ^ 1)
            pairs.append((s * lanes + d, to))
    return lax.ppermute(value, ("section", "dp"), pairs)


def weight_kernel(left, right, *refs):
    core = lax.rem(lax.axis_index("dp"), 2)
    keep, send = refs[-2:]
    half = keep.shape[1]
    both = lax.dot_general(left[...], right[...], TN, preferred_element_type=f32).astype(bf16)
    low, high = both[:half], both[half:]

    @pl.when(core == 0)
    def even():
        keep[0] = low
        send[0] = high

    @pl.when(core != 0)
    def odd():
        keep[0] = high
        send[0] = low


def weight_call(chips, left, right, right_at, units, after):
    total, width = left.shape
    pair = width // chips
    half = pair // 2
    return pl.pallas_call(
        weight_kernel,
        out_shape=[shape_of(chips, half, units)] * 2,
        grid=(chips,),
        in_specs=[
            pl.BlockSpec((total, pair), lambda i: (0, i)),
            pl.BlockSpec((total, units), lambda i: (0, right_at)),
        ]
        + [pl.BlockSpec(memory_space=pl.ANY)] * len(after),
        out_specs=[pl.BlockSpec((1, half, units), lambda i: (i, 0, 0))] * 2,
        compiler_params=pltpu.CompilerParams(vmem_limit_bytes=10 << 20),
        cost_estimate=pl.CostEstimate(
            flops=2 * total * width * units, bytes_accessed=4 * width * units, transcendentals=0
        ),
        name="weight",
    )(left, right, *after)


def from_sides(chip, chips, arrived):
    first = arrived[0][...].astype(f32)
    second = arrived[1][...].astype(f32) if len(arrived) > 1 else first
    even = lax.rem(chip, 2) == 0
    left = jnp.where(chip > 0, jnp.where(even, second, first), 0.0)
    right = jnp.where(chip < chips - 1, jnp.where(even, first, second), 0.0)
    return left, right


def step_kernel(step, chips, keep, swapped, *refs):
    chip = lax.div(lax.axis_index("dp"), 2)
    even = lax.rem(chip, 2) == 0
    outs = refs[-2:]
    arrived = refs[:-2]
    to_right = jnp.clip(chips - step + chip, 0, chips - 1)
    to_left = jnp.clip(step - chips + chip, 0, chips - 1)
    right = keep[to_right].astype(f32) + swapped[to_right].astype(f32)
    left = keep[to_left].astype(f32) + swapped[to_left].astype(f32)
    if arrived:
        from_left, from_right = from_sides(chip, chips, arrived)
        right = right + jnp.where(chip <= step - 1, from_left, 0.0)
        left = left + jnp.where(chip >= chips - step, from_right, 0.0)
    outs[0][...] = jnp.where(even, right, left).astype(bf16)
    outs[1][...] = jnp.where(even, left, right).astype(bf16)


def step_call(step, chips, keep, swapped, arrived):
    half, units = keep.shape[1:]
    return pl.pallas_call(
        functools.partial(step_kernel, step, chips),
        out_shape=[shape_of(half, units)] * 2,
        in_specs=[VM] * (2 + len(arrived)),
        out_specs=[VM, VM],
        compiler_params=pltpu.CompilerParams(vmem_limit_bytes=10 << 20),
        cost_estimate=pl.CostEstimate(flops=half * units, bytes_accessed=half * units, transcendentals=0),
        name="step",
    )(keep, swapped, *arrived)


def final_kernel(chips, keep, swapped, *refs):
    chip = lax.div(lax.axis_index("dp"), 2)
    from_left, from_right = from_sides(chip, chips, refs[:-1])
    refs[-1][...] = keep[chip].astype(f32) + swapped[chip].astype(f32) + from_left + from_right


def final_call(chips, keep, swapped, arrived):
    half, units = keep.shape[1:]
    return pl.pallas_call(
        functools.partial(final_kernel, chips),
        out_shape=shape_of(half, units, dtype=f32),
        in_specs=[VM] * (2 + len(arrived)),
        out_specs=VM,
        compiler_params=pltpu.CompilerParams(vmem_limit_bytes=10 << 20),
        cost_estimate=pl.CostEstimate(flops=half * units, bytes_accessed=half * units, transcendentals=0),
        name="final",
    )(keep, swapped, *arrived)


def body(tokens, cotangent, w_gate, w_up, w_down):
    sections = lax.axis_size("section")
    lanes = lax.axis_size("dp")
    chips = lanes // 2
    total, width = tokens.shape
    units = w_gate.shape[2]
    rows = ROWS
    micro = -(-total // rows)
    last = sections - 1
    arrays = (tokens, cotangent, w_gate[0], w_up[0], w_down[0])

    sent, kept = {}, {}
    arrivals, history = [], []
    for tick in range(micro + 2 * LAG * last):
        routes = plan_routes(tick, micro, sections)
        back = tick - LAG * last
        came = sent.pop(tick - LAG, [])
        saved = []
        for s in range(last):
            index = back - LAG * (last - s)
            if 0 <= index < micro:
                pair, by_place = kept[index + LAG * s]
                saved.append((s, pair + ([] if s == 0 else [by_place[s]])))
        outs, pair, terms = tick_call(
            tick, micro, rows, sections, arrays, [r for _, r in routes], came, saved
        )
        by_place = {s + 1: value for value, route in came for s, what in route if what == "f"}
        kept[tick] = (pair, by_place)
        if terms is not None:
            history.append(terms)
            arrivals.append({s - 1: value for value, route in came for s, what in route if what == "b"})
        sent[tick] = [
            (permute(out, full, sections, lanes), route) for out, (full, route) in zip(outs, routes)
        ]

    laid = functools.partial(collect_call, micro, rows, sections, total)
    all_in = collect_call(micro, rows, sections, total, arrays[1], arrivals)
    all_grad, normed, terms = [laid(None, list(column)) for column in zip(*history)]
    near = [(z, z ^ 1) for z in range(chips)]
    far = [(z, ((z + 1) ^ 1) - 1) for z in range(chips)]
    held = []
    firsts = []

    def begin(which, after):
        left = all_in if which == 0 else normed
        keep, send = weight_call(chips, left, terms, which, units, after)
        held.append((keep, permute(send, {}, sections, lanes)))

    def advance(step, which, arrived):
        keep, swapped = held[which]
        outs = step_call(step, chips, keep, swapped, arrived)
        arrived = [line(outs[0], near, chips)]
        if step > 1 or chips % 2:
            arrived.append(line(outs[1], far, chips))
        return outs[0], arrived

    begin(0, [])
    begin(1, [])
    moving = []
    out, arrived = advance(1, 0, [])
    moving.append(arrived)
    begin(2, [out])
    moving.append(advance(1, 1, [])[1])
    moving.append(advance(1, 2, [])[1])
    for step in range(2, chips):
        for which in range(3):
            moving[which] = advance(step, which, moving[which])[1]
    results = [final_call(chips, *held[which], moving[which]) for which in range(3)]
    grad_d, grad_u, grad_g = results
    return (all_grad[None], grad_g[None], grad_u[None], grad_d[None])


def line(value, pairs, chips):
    route = []
    for z, to in pairs:
        for c in range(2):
            route.append((2 * z + c, 2 * to + c if 0 <= to < chips else 2 * z + 1 - c))
    return lax.ppermute(value, "dp", route)


def solution(mesh):
    placed = (
        P("dp", None),
        P("dp", None),
        P("section", None, None),
        P("section", None, None),
        P("section", None, None),
    )
    return jax.shard_map(
        body,
        mesh=mesh,
        in_specs=placed,
        out_specs=(
            P("section", "dp", None),
            P("section", "dp", None),
            P("section", "dp", None),
            P("section", "dp", None),
        ),
        check_vma=False,
    )
```

```python
import functools

import jax
import jax.numpy as jnp
from jax import lax
from jax.experimental import pallas as pl
from jax.experimental.pallas import tpu as pltpu
from jax.sharding import PartitionSpec as P


ROWS = 48
LAGS_F = (2, 2, 2)
LAGS_B = (2, 2, 2)
PIECES_F = 2
PIECES_B = 2


f32 = jnp.float32
bf16 = jnp.bfloat16
NT = (((1,), (1,)), ((), ()))
TN = (((0,), (0,)), ((), ()))
VM = pl.BlockSpec(memory_space=pltpu.VMEM)


def shape_of(*dims, dtype=bf16):
    return jax.ShapeDtypeStruct(dims, dtype)


def pieces(size, count, body):
    step = size // count
    if count == 1:
        body(pl.ds(0, size))
        return

    def one(i, carry):
        body(pl.ds(pl.multiple_of(i * step, step), step))
        return carry

    lax.fori_loop(0, count, one, 0)


def place_of(start, size):
    return pl.ds(start if isinstance(start, int) else pl.multiple_of(start, size), size)


def pick_of(place, values):
    result = values[0]
    for at, value in enumerate(values[1:]):
        result = jnp.where(place > at, value, result)
    return result


def lag_of(lags, hop):
    return lags[hop] if hop < len(lags) else lags[-1]


def starts_of(sections):
    last = sections - 1
    forward = [0]
    for hop in range(last):
        forward.append(forward[-1] + lag_of(LAGS_F, hop))
    backward = [forward[-1]]
    for hop in range(last):
        backward.append(backward[-1] + lag_of(LAGS_B, hop))
    return forward, backward[::-1]


def tick_kernel(tick, micro, rows, sections, plan, *refs):
    runs_f, runs_b, routes, arrivals, places, inputs, starts_f, starts_b = plan
    refs = list(refs)
    place = lax.axis_index("section")
    tokens = refs.pop(0) if inputs[0] else None
    cotangent = refs.pop(0) if inputs[1] else None
    w_gate, w_up, w_down = refs[:3]
    refs = refs[3:]
    arrived = [(refs.pop(0), takers) for takers in arrivals]
    saved = []
    for at in places:
        saved.append((at, refs[:3]))
        refs = refs[3:]
    outs = [refs.pop(0) for _ in routes]
    if runs_f:
        gate_f, up_f, x_f = refs[:3]
        refs = refs[3:]
    if runs_b:
        new_grad, norms, terms = refs[:3]
        refs = refs[3:]
    x_b, gate_b, up_b, grad_in, normed, hidden, wide = refs
    last = sections - 1
    units = w_gate.shape[1]
    index_f = tick - pick_of(place, starts_f)
    index_b = tick - pick_of(place, starts_b)

    def window(index, source):
        total = source.shape[0]
        start = jnp.clip(index * rows, 0, total - rows)
        return source[pl.ds(pl.multiple_of(start, 16), rows), :]

    good_f = (index_f >= 0) & (index_f < micro)
    good_b = (index_b >= 0) & (index_b < micro)

    def emit(kind, columns, value):
        for out, route in zip(outs, routes):
            senders = [s for s, what in route if what == kind]
            if senders:
                hit = functools.reduce(jnp.logical_or, [place == s for s in senders])

                @pl.when(hit)
                def send():
                    out[:, columns] = value

    def receive(kind, target, source, owner, index):
        if source is not None:

            @pl.when(place == owner)
            def own():
                target[...] = window(index, source)

        for value, takers in arrived:
            for s, what in takers:
                if what == kind:

                    @pl.when(place == s)
                    def passed():
                        target[...] = value[...]

    if runs_f:

        @pl.when(good_f)
        def forward():
            receive("x", x_f, tokens, 0, index_f)
            xf = x_f[...].astype(f32)
            scale = lax.rsqrt(jnp.mean(xf * xf, axis=-1, keepdims=True) + 1e-06)
            normed[...] = (xf * scale).astype(bf16)

            def entry(columns):
                value = normed[...]
                gate = jnp.dot(value, w_gate[:, columns], preferred_element_type=f32)
                upper = jnp.dot(value, w_up[:, columns], preferred_element_type=f32)
                gate_f[:, columns] = gate
                up_f[:, columns] = upper
                value = (gate * jax.nn.sigmoid(gate) * upper).astype(bf16)
                hidden[:, columns] = value

            pieces(units, PIECES_F, entry)

            @pl.when(place != last)
            def exit_():
                def down(columns):
                    branch = lax.dot_general(
                        hidden[...], w_down[columns, :], NT, preferred_element_type=f32
                    )
                    value = (x_f[:, columns].astype(f32) + branch).astype(bf16)
                    emit("x", columns, value)

                pieces(x_f.shape[1], PIECES_F, down)

    if runs_b:

        @pl.when(good_b)
        def backward():
            receive("b", grad_in, cotangent, last, index_b)
            for at, kept in saved:

                @pl.when(place == at)
                def take():
                    gate_b[...] = kept[0][...]
                    up_b[...] = kept[1][...]
                    x_b[...] = kept[2][...]

            if runs_f:

                @pl.when(place == last)
                def same():
                    gate_b[...] = gate_f[...]
                    up_b[...] = up_f[...]
                    x_b[...] = x_f[...]

            def entry(columns):
                d_hidden = jnp.dot(grad_in[...], w_down[:, columns], preferred_element_type=f32)
                gate = gate_b[:, columns]
                upper = up_b[:, columns]
                sig = jax.nn.sigmoid(gate)
                first = columns.start
                size = columns.size
                terms[:, columns] = (gate * sig * upper).astype(bf16)
                d_up = (d_hidden * gate * sig).astype(bf16)
                d_gate = (d_hidden * upper * sig * (1.0 + gate * (1.0 - sig))).astype(bf16)
                terms[:, place_of(units + first, size)] = d_up
                terms[:, place_of(2 * units + first, size)] = d_gate

            pieces(units, PIECES_B, entry)

            def exit_(columns):
                d_norm = lax.dot_general(
                    terms[:, pl.ds(2 * units, units)], w_gate[columns, :], NT, preferred_element_type=f32
                )
                d_norm = d_norm + lax.dot_general(
                    terms[:, pl.ds(units, units)], w_up[columns, :], NT, preferred_element_type=f32
                )
                wide[:, columns] = d_norm

            pieces(x_b.shape[1], PIECES_B, exit_)
            xf = x_b[...].astype(f32)
            scale = lax.rsqrt(jnp.mean(xf * xf, axis=-1, keepdims=True) + 1e-06)
            x_hat = xf * scale
            norms[...] = x_hat.astype(bf16)
            d_norm = wide[...]
            inner = jnp.mean(d_norm * x_hat, axis=-1, keepdims=True)
            grad = grad_in[...].astype(f32) + scale * (d_norm - x_hat * inner)
            grad = grad.astype(bf16)
            new_grad[...] = grad
            emit("b", pl.ds(0, x_b.shape[1]), grad)


def tick_call(tick, micro, rows, sections, arrays, routes, came, saved):
    _, width = arrays[0].shape
    units = arrays[2].shape[1]
    last = sections - 1
    starts_f, starts_b = starts_of(sections)
    runs_f = 0 <= tick < micro + starts_f[last]
    runs_b = 0 <= tick - starts_b[last] < micro + starts_b[0] - starts_b[last]
    own_f = 0 <= tick < micro
    own_b = 0 <= tick - starts_b[last] < micro
    places = [at for at, _ in saved]
    inputs = (own_f, own_b)
    operands = [a for a, used in zip(arrays, inputs) if used] + list(arrays[2:])
    operands += [value for value, _ in came]
    for _, kept in saved:
        operands += kept
    out_shape = [shape_of(rows, width)] * len(routes)
    if runs_f:
        out_shape += [shape_of(rows, units, dtype=f32)] * 2 + [shape_of(rows, width)]
    if runs_b:
        out_shape += [shape_of(rows, width), shape_of(rows, width), shape_of(rows, 3 * units)]
    plan = (
        runs_f,
        runs_b,
        routes,
        [takers for _, takers in came],
        places,
        inputs,
        starts_f,
        starts_b,
    )
    result = pl.pallas_call(
        functools.partial(tick_kernel, tick, micro, rows, sections, plan),
        out_shape=out_shape,
        in_specs=[VM] * len(operands),
        out_specs=[VM] * len(out_shape),
        scratch_shapes=[
            pltpu.VMEM((rows, width), bf16),
            pltpu.VMEM((rows, units), f32),
            pltpu.VMEM((rows, units), f32),
            pltpu.VMEM((rows, width), bf16),
            pltpu.VMEM((rows, width), bf16),
            pltpu.VMEM((rows, units), bf16),
            pltpu.VMEM((rows, width), f32),
        ],
        compiler_params=pltpu.CompilerParams(vmem_limit_bytes=10 << 20),
        cost_estimate=pl.CostEstimate(
            flops=6 * (runs_f + runs_b) * rows * width * units,
            bytes_accessed=6 * width * units,
            transcendentals=0,
        ),
        name="tick",
    )(*operands)
    result = list(result)
    outs = result[: len(routes)]
    rest = result[len(routes) :]
    kept = rest[:3] if runs_f else None
    terms = rest[-3:] if runs_b else None
    return outs, kept, terms


def collect_call(micro, rows, sections, total, whole, sources):
    last = sections - 1
    starts_b = starts_of(sections)[1]
    starts = [min(i * rows, total - rows) for i in range(micro)]
    whole = [] if whole is None else [whole]
    found = []
    at_of = {}
    for tick, value in enumerate(sources):
        by_place = value if isinstance(value, dict) else dict.fromkeys(range(sections), value)
        for at, array in by_place.items():
            known = [i for i, old in enumerate(found) if old is array]
            if not known:
                known = [len(found)]
                found.append(array)
            at_of[tick, at] = known[0]

    def kernel(*refs):
        place = lax.axis_index("section")
        target = refs[-1]
        pool = refs[len(whole) : -1]
        for at in range(sections):

            @pl.when(place == at)
            def take():
                if whole and at == last:
                    target[...] = refs[0][...]
                else:
                    for i, start in enumerate(starts):
                        target[start : start + rows, :] = pool[at_of[i + starts_b[at] - starts_b[last], at]][...]

    operands = whole + found
    width = operands[-1].shape[1]
    return pl.pallas_call(
        kernel,
        out_shape=shape_of(total, width),
        in_specs=[VM] * len(operands),
        out_specs=VM,
        compiler_params=pltpu.CompilerParams(vmem_limit_bytes=10 << 20),
        cost_estimate=pl.CostEstimate(flops=0, bytes_accessed=4 * total * width, transcendentals=0),
        name="collect",
    )(*operands)


def edges_of(sections):
    edges = [("x", at, at + 1) for at in range(sections - 1)]
    return edges + [("b", at, at - 1) for at in range(1, sections)]


def plan_routes(tick, micro, sections):
    starts_f, starts_b = starts_of(sections)
    edges = {}
    for kind, a, b in edges_of(sections):
        start = (starts_b if kind == "b" else starts_f)[a]
        if 0 <= tick - start < micro:
            edges[a, b] = kind
    plans = []
    both = [(a, b) for a, b in edges if a < b and (b, a) in edges]
    for parity in (0, 1):
        chosen = [p for a, b in both if a % 2 == parity for p in ((a, b), (b, a))]
        if chosen:
            plans.append({pair: edges.pop(pair) for pair in chosen})
    for kind in ("x", "b"):
        chosen = [pair for pair, what in edges.items() if what == kind]
        if chosen:
            plans.append({pair: kind for pair in chosen})
    routes = []
    for plan in plans:
        full = dict(plan)
        full = {a: b for a, b in full}
        targets = set(full.values())
        for a in sorted(full):
            if a not in targets:
                end = a
                while end in full:
                    end = full[end]
                full[end] = a
        routes.append((full, [(kind, a, b) for (a, b), kind in plan.items()]))
    return routes


def permute(value, full, sections, lanes):
    pairs = []
    for s in range(sections):
        for d in range(lanes):
            to = full[s] * lanes + d if s in full else s * lanes + (d ^ 1)
            pairs.append((s * lanes + d, to))
    return lax.ppermute(value, ("section", "dp"), pairs)


def weight_kernel(left, right, *refs):
    core = lax.rem(lax.axis_index("dp"), 2)
    keep, send = refs[-2:]
    half = keep.shape[1]
    both = lax.dot_general(left[...], right[...], TN, preferred_element_type=f32).astype(bf16)
    low, high = both[:half], both[half:]

    @pl.when(core == 0)
    def even():
        keep[0] = low
        send[0] = high

    @pl.when(core != 0)
    def odd():
        keep[0] = high
        send[0] = low


def weight_call(chips, left, right, right_at, units, after):
    total, width = left.shape
    pair = width // chips
    half = pair // 2
    return pl.pallas_call(
        weight_kernel,
        out_shape=[shape_of(chips, half, units)] * 2,
        grid=(chips,),
        in_specs=[
            pl.BlockSpec((total, pair), lambda i: (0, i)),
            pl.BlockSpec((total, units), lambda i: (0, right_at)),
        ]
        + [pl.BlockSpec(memory_space=pl.ANY)] * len(after),
        out_specs=[pl.BlockSpec((1, half, units), lambda i: (i, 0, 0))] * 2,
        compiler_params=pltpu.CompilerParams(vmem_limit_bytes=10 << 20),
        cost_estimate=pl.CostEstimate(
            flops=2 * total * width * units, bytes_accessed=4 * width * units, transcendentals=0
        ),
        name="weight",
    )(left, right, *after)


def from_sides(chip, chips, arrived):
    first = arrived[0][...].astype(f32)
    second = arrived[1][...].astype(f32) if len(arrived) > 1 else first
    even = lax.rem(chip, 2) == 0
    left = jnp.where(chip > 0, jnp.where(even, second, first), 0.0)
    right = jnp.where(chip < chips - 1, jnp.where(even, first, second), 0.0)
    return left, right


def step_kernel(step, chips, keep, swapped, *refs):
    chip = lax.div(lax.axis_index("dp"), 2)
    even = lax.rem(chip, 2) == 0
    outs = refs[-2:]
    arrived = refs[:-2]
    to_right = jnp.clip(chips - step + chip, 0, chips - 1)
    to_left = jnp.clip(step - chips + chip, 0, chips - 1)
    right = keep[to_right].astype(f32) + swapped[to_right].astype(f32)
    left = keep[to_left].astype(f32) + swapped[to_left].astype(f32)
    if arrived:
        from_left, from_right = from_sides(chip, chips, arrived)
        right = right + jnp.where(chip <= step - 1, from_left, 0.0)
        left = left + jnp.where(chip >= chips - step, from_right, 0.0)
    outs[0][...] = jnp.where(even, right, left).astype(bf16)
    outs[1][...] = jnp.where(even, left, right).astype(bf16)


def step_call(step, chips, keep, swapped, arrived):
    half, units = keep.shape[1:]
    return pl.pallas_call(
        functools.partial(step_kernel, step, chips),
        out_shape=[shape_of(half, units)] * 2,
        in_specs=[VM] * (2 + len(arrived)),
        out_specs=[VM, VM],
        compiler_params=pltpu.CompilerParams(vmem_limit_bytes=10 << 20),
        cost_estimate=pl.CostEstimate(flops=half * units, bytes_accessed=half * units, transcendentals=0),
        name="step",
    )(keep, swapped, *arrived)


def final_kernel(chips, keep, swapped, *refs):
    chip = lax.div(lax.axis_index("dp"), 2)
    from_left, from_right = from_sides(chip, chips, refs[:-1])
    refs[-1][...] = keep[chip].astype(f32) + swapped[chip].astype(f32) + from_left + from_right


def final_call(chips, keep, swapped, arrived):
    half, units = keep.shape[1:]
    return pl.pallas_call(
        functools.partial(final_kernel, chips),
        out_shape=shape_of(half, units, dtype=f32),
        in_specs=[VM] * (2 + len(arrived)),
        out_specs=VM,
        compiler_params=pltpu.CompilerParams(vmem_limit_bytes=10 << 20),
        cost_estimate=pl.CostEstimate(flops=half * units, bytes_accessed=half * units, transcendentals=0),
        name="final",
    )(keep, swapped, *arrived)


def body(tokens, cotangent, w_gate, w_up, w_down):
    sections = lax.axis_size("section")
    lanes = lax.axis_size("dp")
    chips = lanes // 2
    total, _ = tokens.shape
    units = w_gate.shape[2]
    rows = ROWS
    micro = -(-total // rows)
    last = sections - 1
    arrays = (tokens, cotangent, w_gate[0], w_up[0], w_down[0])

    starts_f, starts_b = starts_of(sections)
    sent, kept = {}, {}
    arrivals, history = [], []
    for tick in range(micro + starts_b[0]):
        routes = plan_routes(tick, micro, sections)
        came, into = [], {}
        for kind, a, b in edges_of(sections):
            starts = starts_b if kind == "b" else starts_f
            if 0 <= tick - starts[b] < micro:
                value = sent[kind, a, b, tick - starts[b] + starts[a]]
                takers = [old for array, old in came if array is value]
                if not takers:
                    takers = [[]]
                    came.append((value, takers[0]))
                takers[0].append((b, kind))
                if kind == "b":
                    into[b] = value
        saved = []
        for at in range(last):
            index = tick - starts_b[at]
            if 0 <= index < micro:
                saved.append((at, kept[index + starts_f[at]]))
        outs, kept[tick], terms = tick_call(
            tick,
            micro,
            rows,
            sections,
            arrays,
            [[(a, kind) for kind, a, _ in taken] for _, taken in routes],
            came,
            saved,
        )
        if terms is not None:
            history.append(terms)
            arrivals.append(into)
        for out, (full, taken) in zip(outs, routes):
            value = permute(out, full, sections, lanes)
            for kind, a, b in taken:
                sent[kind, a, b, tick] = value

    laid = functools.partial(collect_call, micro, rows, sections, total)
    all_in = collect_call(micro, rows, sections, total, arrays[1], arrivals)
    all_grad, normed, terms = [laid(None, list(column)) for column in zip(*history)]
    near = [(z, z ^ 1) for z in range(chips)]
    far = [(z, ((z + 1) ^ 1) - 1) for z in range(chips)]
    held = []

    def begin(which, after):
        left = all_in if which == 0 else normed
        keep, send = weight_call(chips, left, terms, which, units, after)
        held.append((keep, permute(send, {}, sections, lanes)))

    def advance(step, which, arrived):
        keep, swapped = held[which]
        outs = step_call(step, chips, keep, swapped, arrived)
        arrived = [line(outs[0], near, chips)]
        if step > 1 or chips % 2:
            arrived.append(line(outs[1], far, chips))
        return outs[0], arrived

    begin(0, [])
    begin(1, [])
    moving = []
    out, arrived = advance(1, 0, [])
    moving.append(arrived)
    begin(2, [out])
    moving.append(advance(1, 1, [])[1])
    moving.append(advance(1, 2, [])[1])
    for step in range(2, chips):
        for which in range(3):
            moving[which] = advance(step, which, moving[which])[1]
    results = [final_call(chips, *held[which], moving[which]) for which in range(3)]
    grad_d, grad_u, grad_g = results
    return (all_grad[None], grad_g[None], grad_u[None], grad_d[None])


def line(value, pairs, chips):
    route = []
    for z, to in pairs:
        for c in range(2):
            route.append((2 * z + c, 2 * to + c if 0 <= to < chips else 2 * z + 1 - c))
    return lax.ppermute(value, "dp", route)


def solution(mesh):
    placed = (
        P("dp", None),
        P("dp", None),
        P("section", None, None),
        P("section", None, None),
        P("section", None, None),
    )
    return jax.shard_map(
        body,
        mesh=mesh,
        in_specs=placed,
        out_specs=(
            P("section", "dp", None),
            P("section", "dp", None),
            P("section", "dp", None),
            P("section", "dp", None),
        ),
        check_vma=False,
    )
```

```python
import functools

import jax
import jax.numpy as jnp
from jax import lax
from jax.experimental import pallas as pl
from jax.experimental.pallas import tpu as pltpu
from jax.sharding import PartitionSpec as P


ROWS = 48
LAGS_F = (2, 2, 2)
LAGS_B = (2, 2, 2)
LOAD_MIB = 44
PIECES_F = 2
PIECES_B = 2


f32 = jnp.float32
bf16 = jnp.bfloat16
NT = (((1,), (1,)), ((), ()))
TN = (((0,), (0,)), ((), ()))
VM = pl.BlockSpec(memory_space=pltpu.VMEM)
ANY = pl.BlockSpec(memory_space=pl.ANY)


def shape_of(*dims, dtype=bf16):
    return jax.ShapeDtypeStruct(dims, dtype)


def pieces(size, count, body):
    step = size // count
    if count == 1:
        body(pl.ds(0, size))
        return

    def one(i, carry):
        body(pl.ds(pl.multiple_of(i * step, step), step))
        return carry

    lax.fori_loop(0, count, one, 0)


def place_of(start, size):
    return pl.ds(start if isinstance(start, int) else pl.multiple_of(start, size), size)


def pick_of(place, values):
    result = values[0]
    for at, value in enumerate(values[1:]):
        result = jnp.where(place > at, value, result)
    return result


def lag_of(lags, hop):
    return lags[hop] if hop < len(lags) else lags[-1]


def starts_of(sections):
    last = sections - 1
    forward = [0]
    for hop in range(last):
        forward.append(forward[-1] + lag_of(LAGS_F, hop))
    backward = [forward[-1]]
    for hop in range(last):
        backward.append(backward[-1] + lag_of(LAGS_B, hop))
    return forward, backward[::-1]


def tick_kernel(tick, micro, rows, sections, plan, *refs):
    runs_f, runs_b, routes, arrivals, places, inputs, starts_f, starts_b, loading = plan
    refs = list(refs)
    place = lax.axis_index("section")
    tokens = refs.pop(0) if inputs[0] else None
    cotangent = refs.pop(0) if inputs[1] else None
    w_gate, w_up, w_down = refs[:3]
    refs = refs[3:]
    loads = []
    if loading:
        sems = refs.pop()
        sources = [tokens.at[pl.ds(0, rows), :], w_gate, w_up, w_down]
    arrived = [(refs.pop(0), takers) for takers in arrivals]
    saved = []
    for at in places:
        saved.append((at, refs[:3]))
        refs = refs[3:]
    outs = [refs.pop(0) for _ in routes]
    if runs_f:
        gate_f, up_f, x_f = refs[:3]
        refs = refs[3:]
    if runs_b:
        new_grad, norms, terms = refs[:3]
        refs = refs[3:]
    if loading:
        w_gate, w_up, w_down = refs[:3]
        refs = refs[3:]
        targets = [x_f, w_gate, w_up, w_down]
        for number in range(4):
            copy = pltpu.make_async_copy(sources[number], targets[number], sems.at[number])
            copy.start()
            loads.append(copy)
    x_b, gate_b, up_b, grad_in, normed, hidden, wide = refs
    last = sections - 1
    units = w_gate.shape[1]
    index_f = tick - pick_of(place, starts_f)
    index_b = tick - pick_of(place, starts_b)

    def window(index, source):
        total = source.shape[0]
        start = jnp.clip(index * rows, 0, total - rows)
        return source[pl.ds(pl.multiple_of(start, 16), rows), :]

    good_f = (index_f >= 0) & (index_f < micro)
    good_b = (index_b >= 0) & (index_b < micro)

    def emit(kind, columns, value):
        for out, route in zip(outs, routes):
            senders = [s for s, what in route if what == kind]
            if senders:
                hit = functools.reduce(jnp.logical_or, [place == s for s in senders])

                @pl.when(hit)
                def send():
                    out[:, columns] = value

    def receive(kind, target, source, owner, index):
        if source is not None:

            @pl.when(place == owner)
            def own():
                target[...] = window(index, source)

        for value, takers in arrived:
            for s, what in takers:
                if what == kind:

                    @pl.when(place == s)
                    def passed():
                        target[...] = value[...]

    if runs_f:

        @pl.when(good_f)
        def forward():
            if loading:
                loads[0].wait()
            else:
                receive("x", x_f, tokens, 0, index_f)
            xf = x_f[...].astype(f32)
            scale = lax.rsqrt(jnp.mean(xf * xf, axis=-1, keepdims=True) + 1e-06)
            normed[...] = (xf * scale).astype(bf16)

            def entry(columns):
                value = normed[...]
                gate = jnp.dot(value, w_gate[:, columns], preferred_element_type=f32)
                upper = jnp.dot(value, w_up[:, columns], preferred_element_type=f32)
                gate_f[:, columns] = gate
                up_f[:, columns] = upper
                value = (gate * jax.nn.sigmoid(gate) * upper).astype(bf16)
                hidden[:, columns] = value

            for copy in loads[1:3]:
                copy.wait()
            pieces(units, PIECES_F, entry)
            for copy in loads[3:]:
                copy.wait()

            @pl.when(place != last)
            def exit_():
                def down(columns):
                    branch = lax.dot_general(
                        hidden[...], w_down[columns, :], NT, preferred_element_type=f32
                    )
                    value = (x_f[:, columns].astype(f32) + branch).astype(bf16)
                    emit("x", columns, value)

                pieces(x_f.shape[1], PIECES_F, down)

    if loading:

        @pl.when(jnp.logical_not(good_f))
        def idle():
            for copy in loads:
                copy.wait()

    if runs_b:

        @pl.when(good_b)
        def backward():
            receive("b", grad_in, cotangent, last, index_b)
            for at, kept in saved:

                @pl.when(place == at)
                def take():
                    gate_b[...] = kept[0][...]
                    up_b[...] = kept[1][...]
                    x_b[...] = kept[2][...]

            if runs_f:

                @pl.when(place == last)
                def same():
                    gate_b[...] = gate_f[...]
                    up_b[...] = up_f[...]
                    x_b[...] = x_f[...]

            def entry(columns):
                d_hidden = jnp.dot(grad_in[...], w_down[:, columns], preferred_element_type=f32)
                gate = gate_b[:, columns]
                upper = up_b[:, columns]
                sig = jax.nn.sigmoid(gate)
                first = columns.start
                size = columns.size
                terms[:, columns] = (gate * sig * upper).astype(bf16)
                d_up = (d_hidden * gate * sig).astype(bf16)
                d_gate = (d_hidden * upper * sig * (1.0 + gate * (1.0 - sig))).astype(bf16)
                terms[:, place_of(units + first, size)] = d_up
                terms[:, place_of(2 * units + first, size)] = d_gate

            pieces(units, PIECES_B, entry)

            def exit_(columns):
                d_norm = lax.dot_general(
                    terms[:, pl.ds(2 * units, units)], w_gate[columns, :], NT, preferred_element_type=f32
                )
                d_norm = d_norm + lax.dot_general(
                    terms[:, pl.ds(units, units)], w_up[columns, :], NT, preferred_element_type=f32
                )
                wide[:, columns] = d_norm

            pieces(x_b.shape[1], PIECES_B, exit_)
            xf = x_b[...].astype(f32)
            scale = lax.rsqrt(jnp.mean(xf * xf, axis=-1, keepdims=True) + 1e-06)
            x_hat = xf * scale
            norms[...] = x_hat.astype(bf16)
            d_norm = wide[...]
            inner = jnp.mean(d_norm * x_hat, axis=-1, keepdims=True)
            grad = grad_in[...].astype(f32) + scale * (d_norm - x_hat * inner)
            grad = grad.astype(bf16)
            new_grad[...] = grad
            emit("b", pl.ds(0, x_b.shape[1]), grad)


def tick_call(tick, micro, rows, sections, arrays, routes, came, saved):
    _, width = arrays[0].shape
    units = arrays[2].shape[1]
    last = sections - 1
    starts_f, starts_b = starts_of(sections)
    runs_f = 0 <= tick < micro + starts_f[last]
    runs_b = 0 <= tick - starts_b[last] < micro + starts_b[0] - starts_b[last]
    own_f = 0 <= tick < micro
    own_b = 0 <= tick - starts_b[last] < micro
    places = [at for at, _ in saved]
    inputs = (own_f, own_b)
    operands = [a for a, used in zip(arrays, inputs) if used] + list(arrays[2:])
    operands += [value for value, _ in came]
    for _, kept in saved:
        operands += kept
    out_shape = [shape_of(rows, width)] * len(routes)
    if runs_f:
        out_shape += [shape_of(rows, units, dtype=f32)] * 2 + [shape_of(rows, width)]
    if runs_b:
        out_shape += [shape_of(rows, width), shape_of(rows, width), shape_of(rows, 3 * units)]
    loading = tick == 0
    if loading:
        out_shape += [shape_of(*w.shape) for w in arrays[2:]]
    plan = (
        runs_f,
        runs_b,
        routes,
        [takers for _, takers in came],
        places,
        inputs,
        starts_f,
        starts_b,
        loading,
    )
    result = pl.pallas_call(
        functools.partial(tick_kernel, tick, micro, rows, sections, plan),
        out_shape=out_shape,
        in_specs=[ANY if loading else VM] * len(operands),
        out_specs=[VM] * len(out_shape),
        scratch_shapes=[
            pltpu.VMEM((rows, width), bf16),
            pltpu.VMEM((rows, units), f32),
            pltpu.VMEM((rows, units), f32),
            pltpu.VMEM((rows, width), bf16),
            pltpu.VMEM((rows, width), bf16),
            pltpu.VMEM((rows, units), bf16),
            pltpu.VMEM((rows, width), f32),
        ]
        + [pltpu.SemaphoreType.DMA((4,))] * loading,
        compiler_params=pltpu.CompilerParams(vmem_limit_bytes=(LOAD_MIB if loading else 10) << 20),
        cost_estimate=pl.CostEstimate(
            flops=6 * (runs_f + runs_b) * rows * width * units,
            bytes_accessed=6 * width * units,
            transcendentals=0,
        ),
        name="tick",
    )(*operands)
    result = list(result)
    outs = result[: len(routes)]
    rest = result[len(routes) :]
    loaded = None
    if loading:
        rest, loaded = rest[:-3], rest[-3:]
    kept = rest[:3] if runs_f else None
    terms = rest[-3:] if runs_b else None
    return outs, kept, terms, loaded


def collect_call(micro, rows, sections, total, whole, sources):
    last = sections - 1
    starts_b = starts_of(sections)[1]
    starts = [min(i * rows, total - rows) for i in range(micro)]
    whole = [] if whole is None else [whole]
    found = []
    at_of = {}
    for tick, value in enumerate(sources):
        by_place = value if isinstance(value, dict) else dict.fromkeys(range(sections), value)
        for at, array in by_place.items():
            known = [i for i, old in enumerate(found) if old is array]
            if not known:
                known = [len(found)]
                found.append(array)
            at_of[tick, at] = known[0]

    def kernel(*refs):
        place = lax.axis_index("section")
        target = refs[-1]
        pool = refs[len(whole) : -1]
        for at in range(sections):

            @pl.when(place == at)
            def take():
                if whole and at == last:
                    target[...] = refs[0][...]
                else:
                    for i, start in enumerate(starts):
                        target[start : start + rows, :] = pool[at_of[i + starts_b[at] - starts_b[last], at]][...]

    operands = whole + found
    width = operands[-1].shape[1]
    return pl.pallas_call(
        kernel,
        out_shape=shape_of(total, width),
        in_specs=[VM] * len(operands),
        out_specs=VM,
        compiler_params=pltpu.CompilerParams(vmem_limit_bytes=10 << 20),
        cost_estimate=pl.CostEstimate(flops=0, bytes_accessed=4 * total * width, transcendentals=0),
        name="collect",
    )(*operands)


def edges_of(sections):
    edges = [("x", at, at + 1) for at in range(sections - 1)]
    return edges + [("b", at, at - 1) for at in range(1, sections)]


def plan_routes(tick, micro, sections):
    starts_f, starts_b = starts_of(sections)
    edges = {}
    for kind, a, b in edges_of(sections):
        start = (starts_b if kind == "b" else starts_f)[a]
        if 0 <= tick - start < micro:
            edges[a, b] = kind
    plans = []
    both = [(a, b) for a, b in edges if a < b and (b, a) in edges]
    for parity in (0, 1):
        chosen = [p for a, b in both if a % 2 == parity for p in ((a, b), (b, a))]
        if chosen:
            plans.append({pair: edges.pop(pair) for pair in chosen})
    for kind in ("x", "b"):
        chosen = [pair for pair, what in edges.items() if what == kind]
        if chosen:
            plans.append({pair: kind for pair in chosen})
    routes = []
    for plan in plans:
        full = dict(plan)
        full = {a: b for a, b in full}
        targets = set(full.values())
        for a in sorted(full):
            if a not in targets:
                end = a
                while end in full:
                    end = full[end]
                full[end] = a
        routes.append((full, [(kind, a, b) for (a, b), kind in plan.items()]))
    return routes


def permute(value, full, sections, lanes):
    pairs = []
    for s in range(sections):
        for d in range(lanes):
            to = full[s] * lanes + d if s in full else s * lanes + (d ^ 1)
            pairs.append((s * lanes + d, to))
    return lax.ppermute(value, ("section", "dp"), pairs)


def weight_kernel(left, right, *refs):
    core = lax.rem(lax.axis_index("dp"), 2)
    keep, send = refs[-2:]
    half = keep.shape[1]
    both = lax.dot_general(left[...], right[...], TN, preferred_element_type=f32).astype(bf16)
    low, high = both[:half], both[half:]

    @pl.when(core == 0)
    def even():
        keep[0] = low
        send[0] = high

    @pl.when(core != 0)
    def odd():
        keep[0] = high
        send[0] = low


def weight_call(chips, left, right, right_at, units, after, ends=False):
    total, width = left.shape
    pair = width // chips
    half = pair // 2
    count = 2 if ends else chips

    def column(i):
        return (0, (chips - 1) * (1 - i) if ends else i)

    return pl.pallas_call(
        weight_kernel,
        out_shape=[shape_of(count, half, units)] * 2,
        grid=(count,),
        in_specs=[
            pl.BlockSpec((total, pair), column),
            pl.BlockSpec((total, units), lambda i: (0, right_at)),
        ]
        + [pl.BlockSpec(memory_space=pl.ANY)] * len(after),
        out_specs=[pl.BlockSpec((1, half, units), lambda i: (i, 0, 0))] * 2,
        compiler_params=pltpu.CompilerParams(vmem_limit_bytes=10 << 20),
        cost_estimate=pl.CostEstimate(
            flops=2 * total * pair * count * units,
            bytes_accessed=4 * pair * count * units,
            transcendentals=0,
        ),
        name="weight",
    )(left, right, *after)


def from_sides(chip, chips, arrived):
    first = arrived[0][...].astype(f32)
    second = arrived[1][...].astype(f32) if len(arrived) > 1 else first
    even = lax.rem(chip, 2) == 0
    left = jnp.where(chip > 0, jnp.where(even, second, first), 0.0)
    right = jnp.where(chip < chips - 1, jnp.where(even, first, second), 0.0)
    return left, right


def step_kernel(step, chips, keep, swapped, *refs):
    chip = lax.div(lax.axis_index("dp"), 2)
    even = lax.rem(chip, 2) == 0
    outs = refs[-2:]
    arrived = refs[:-2]
    if keep.shape[0] < chips:
        to_right, to_left = 0, 1
    else:
        to_right = jnp.clip(chips - step + chip, 0, chips - 1)
        to_left = jnp.clip(step - chips + chip, 0, chips - 1)
    right = keep[to_right].astype(f32) + swapped[to_right].astype(f32)
    left = keep[to_left].astype(f32) + swapped[to_left].astype(f32)
    if arrived:
        from_left, from_right = from_sides(chip, chips, arrived)
        right = right + jnp.where(chip <= step - 1, from_left, 0.0)
        left = left + jnp.where(chip >= chips - step, from_right, 0.0)
    outs[0][...] = jnp.where(even, right, left).astype(bf16)
    outs[1][...] = jnp.where(even, left, right).astype(bf16)


def step_call(step, chips, keep, swapped, arrived):
    half, units = keep.shape[1:]
    return pl.pallas_call(
        functools.partial(step_kernel, step, chips),
        out_shape=[shape_of(half, units)] * 2,
        in_specs=[VM] * (2 + len(arrived)),
        out_specs=[VM, VM],
        compiler_params=pltpu.CompilerParams(vmem_limit_bytes=10 << 20),
        cost_estimate=pl.CostEstimate(flops=half * units, bytes_accessed=half * units, transcendentals=0),
        name="step",
    )(keep, swapped, *arrived)


def final_kernel(chips, keep, swapped, *refs):
    chip = lax.div(lax.axis_index("dp"), 2)
    from_left, from_right = from_sides(chip, chips, refs[:-1])
    refs[-1][...] = keep[chip].astype(f32) + swapped[chip].astype(f32) + from_left + from_right


def final_call(chips, keep, swapped, arrived):
    half, units = keep.shape[1:]
    return pl.pallas_call(
        functools.partial(final_kernel, chips),
        out_shape=shape_of(half, units, dtype=f32),
        in_specs=[VM] * (2 + len(arrived)),
        out_specs=VM,
        compiler_params=pltpu.CompilerParams(vmem_limit_bytes=10 << 20),
        cost_estimate=pl.CostEstimate(flops=half * units, bytes_accessed=half * units, transcendentals=0),
        name="final",
    )(keep, swapped, *arrived)


def body(tokens, cotangent, w_gate, w_up, w_down):
    sections = lax.axis_size("section")
    lanes = lax.axis_size("dp")
    chips = lanes // 2
    total, _ = tokens.shape
    units = w_gate.shape[2]
    rows = ROWS
    micro = -(-total // rows)
    last = sections - 1
    arrays = (tokens, cotangent, w_gate[0], w_up[0], w_down[0])

    starts_f, starts_b = starts_of(sections)
    sent, kept = {}, {}
    arrivals, history = [], []
    for tick in range(micro + starts_b[0]):
        routes = plan_routes(tick, micro, sections)
        came, into = [], {}
        for kind, a, b in edges_of(sections):
            starts = starts_b if kind == "b" else starts_f
            if 0 <= tick - starts[b] < micro:
                value = sent[kind, a, b, tick - starts[b] + starts[a]]
                takers = [old for array, old in came if array is value]
                if not takers:
                    takers = [[]]
                    came.append((value, takers[0]))
                takers[0].append((b, kind))
                if kind == "b":
                    into[b] = value
        saved = []
        for at in range(last):
            index = tick - starts_b[at]
            if 0 <= index < micro:
                saved.append((at, kept[index + starts_f[at]]))
        outs, kept[tick], terms, loaded = tick_call(
            tick,
            micro,
            rows,
            sections,
            arrays,
            [[(a, kind) for kind, a, _ in taken] for _, taken in routes],
            came,
            saved,
        )
        if loaded is not None:
            arrays = (tokens, cotangent, *loaded)
        if terms is not None:
            history.append(terms)
            arrivals.append(into)
        for out, (full, taken) in zip(outs, routes):
            value = permute(out, full, sections, lanes)
            for kind, a, b in taken:
                sent[kind, a, b, tick] = value

    laid = functools.partial(collect_call, micro, rows, sections, total)
    all_in = collect_call(micro, rows, sections, total, arrays[1], arrivals)
    all_grad, normed, terms = [laid(None, list(column)) for column in zip(*history)]
    near = [(z, z ^ 1) for z in range(chips)]
    far = [(z, ((z + 1) ^ 1) - 1) for z in range(chips)]
    held = {}

    def begin(which, after):
        left = all_in if which == 0 else normed
        keep, send = weight_call(chips, left, terms, which, units, after)
        held[which] = (keep, permute(send, {}, sections, lanes))

    def advance(step, which, arrived, quick=None):
        keep, swapped = quick or held[which]
        outs = step_call(step, chips, keep, swapped, arrived)
        arrived = [line(outs[0], near, chips)]
        if step > 1 or chips % 2:
            arrived.append(line(outs[1], far, chips))
        return outs[0], arrived

    keep, send = weight_call(chips, all_in, terms, 0, units, [], True)
    quick = (keep, permute(send, {}, sections, lanes))
    begin(1, [send])
    moving = {}
    out, moving[0] = advance(1, 0, [], quick)
    begin(2, [out])
    out, moving[1] = advance(1, 1, [])
    begin(0, [out])
    moving[2] = advance(1, 2, [])[1]
    for step in range(2, chips):
        for which in range(3):
            moving[which] = advance(step, which, moving[which])[1]
    results = [final_call(chips, *held[which], moving[which]) for which in range(3)]
    grad_d, grad_u, grad_g = results
    return (all_grad[None], grad_g[None], grad_u[None], grad_d[None])


def line(value, pairs, chips):
    route = []
    for z, to in pairs:
        for c in range(2):
            route.append((2 * z + c, 2 * to + c if 0 <= to < chips else 2 * z + 1 - c))
    return lax.ppermute(value, "dp", route)


def solution(mesh):
    placed = (
        P("dp", None),
        P("dp", None),
        P("section", None, None),
        P("section", None, None),
        P("section", None, None),
    )
    return jax.shard_map(
        body,
        mesh=mesh,
        in_specs=placed,
        out_specs=(
            P("section", "dp", None),
            P("section", "dp", None),
            P("section", "dp", None),
            P("section", "dp", None),
        ),
        check_vma=False,
    )
```

```python
import functools

import jax
import jax.numpy as jnp
from jax import lax
from jax.experimental import pallas as pl
from jax.experimental.pallas import tpu as pltpu
from jax.sharding import PartitionSpec as P


ROWS = 48
LAGS_F = (2, 2, 2)
LAGS_B = (2, 2, 2)
LOAD_MIB = 44
PIECES_F = 2
PIECES_B = 2


f32 = jnp.float32
bf16 = jnp.bfloat16
NT = (((1,), (1,)), ((), ()))
TN = (((0,), (0,)), ((), ()))
VM = pl.BlockSpec(memory_space=pltpu.VMEM)
ANY = pl.BlockSpec(memory_space=pl.ANY)


def shape_of(*dims, dtype=bf16):
    return jax.ShapeDtypeStruct(dims, dtype)


def pieces(size, count, body):
    step = size // count
    if count == 1:
        body(pl.ds(0, size))
        return

    def one(i, carry):
        body(pl.ds(pl.multiple_of(i * step, step), step))
        return carry

    lax.fori_loop(0, count, one, 0)


def place_of(start, size):
    return pl.ds(start if isinstance(start, int) else pl.multiple_of(start, size), size)


def pick_of(place, values):
    result = values[0]
    for at, value in enumerate(values[1:]):
        result = jnp.where(place > at, value, result)
    return result


def lag_of(lags, hop):
    return lags[hop] if hop < len(lags) else lags[-1]


def starts_of(sections):
    last = sections - 1
    forward = [0]
    for hop in range(last):
        forward.append(forward[-1] + lag_of(LAGS_F, hop))
    backward = [forward[-1]]
    for hop in range(last):
        backward.append(backward[-1] + lag_of(LAGS_B, hop))
    return forward, backward[::-1]


def tick_kernel(tick, micro, rows, sections, plan, *refs):
    runs_f, runs_b, routes, arrivals, places, inputs, starts_f, starts_b, loading, defer = plan
    refs = list(refs)
    place = lax.axis_index("section")
    tokens = refs.pop(0) if inputs[0] else None
    cotangent = refs.pop(0) if inputs[1] else None
    w_gate, w_up, w_down = refs[:3]
    refs = refs[3:]
    loads = []
    if loading:
        sems = refs.pop()
        sources = [tokens.at[pl.ds(0, rows), :], w_gate, w_up, w_down]
    arrived = [(refs.pop(0), takers) for takers in arrivals]
    saved = []
    for at in places:
        saved.append((at, refs[:3]))
        refs = refs[3:]
    outs = [refs.pop(0) for _ in routes]
    if runs_f:
        gate_f, up_f, x_f = refs[:3]
        refs = refs[3:]
    if runs_b:
        new_grad, norms, terms = refs[:3]
        refs = refs[3:]
    if loading:
        w_gate, w_up, w_down = refs[:3]
        refs = refs[3:]
        targets = [x_f, w_gate, w_up, w_down]
        for number in range(4):
            copy = pltpu.make_async_copy(sources[number], targets[number], sems.at[number])
            copy.start()
            loads.append(copy)
    x_b, gate_b, up_b, grad_in, normed, hidden, wide = refs
    last = sections - 1
    units = w_gate.shape[1]
    index_f = tick - pick_of(place, starts_f)
    index_b = tick - pick_of(place, starts_b)

    def window(index, source):
        total = source.shape[0]
        start = jnp.clip(index * rows, 0, total - rows)
        return source[pl.ds(pl.multiple_of(start, 16), rows), :]

    good_f = (index_f >= 0) & (index_f < micro)
    good_b = (index_b >= 0) & (index_b < micro)

    def emit(kind, columns, value):
        for out, route in zip(outs, routes):
            senders = [s for s, what in route if what == kind]
            if senders:
                hit = functools.reduce(jnp.logical_or, [place == s for s in senders])

                @pl.when(hit)
                def send():
                    out[:, columns] = value

    def receive(kind, target, source, owner, index):
        if source is not None:

            @pl.when(place == owner)
            def own():
                target[...] = window(index, source)

        for value, takers in arrived:
            for s, what in takers:
                if what == kind:

                    @pl.when(place == s)
                    def passed():
                        target[...] = value[...]

    if runs_f:

        @pl.when(good_f)
        def forward():
            if loading:
                loads[0].wait()
            else:
                receive("x", x_f, tokens, 0, index_f)
            xf = x_f[...].astype(f32)
            scale = lax.rsqrt(jnp.mean(xf * xf, axis=-1, keepdims=True) + 1e-06)
            normed[...] = (xf * scale).astype(bf16)

            def entry(columns):
                value = normed[...]
                gate = jnp.dot(value, w_gate[:, columns], preferred_element_type=f32)
                upper = jnp.dot(value, w_up[:, columns], preferred_element_type=f32)
                gate_f[:, columns] = gate
                up_f[:, columns] = upper
                value = (gate * jax.nn.sigmoid(gate) * upper).astype(bf16)
                hidden[:, columns] = value

            for copy in loads[1:3]:
                copy.wait()
            pieces(units, PIECES_F, entry)
            for copy in loads[3:]:
                copy.wait()

            @pl.when(place != last)
            def exit_():
                def down(columns):
                    branch = lax.dot_general(
                        hidden[...], w_down[columns, :], NT, preferred_element_type=f32
                    )
                    value = (x_f[:, columns].astype(f32) + branch).astype(bf16)
                    emit("x", columns, value)

                pieces(x_f.shape[1], PIECES_F, down)

    if loading:

        @pl.when(jnp.logical_not(good_f))
        def idle():
            for copy in loads:
                copy.wait()

    if runs_b:

        @pl.when(good_b)
        def backward():
            receive("b", grad_in, cotangent, last, index_b)
            for at, kept in saved:

                @pl.when(place == at)
                def take():
                    gate_b[...] = kept[0][...]
                    up_b[...] = kept[1][...]
                    x_b[...] = kept[2][...]

            if runs_f:

                @pl.when(place == last)
                def same():
                    gate_b[...] = gate_f[...]
                    up_b[...] = up_f[...]
                    x_b[...] = x_f[...]

            def entry(columns):
                d_hidden = jnp.dot(grad_in[...], w_down[:, columns], preferred_element_type=f32)
                gate = gate_b[:, columns]
                upper = up_b[:, columns]
                sig = jax.nn.sigmoid(gate)
                first = columns.start
                size = columns.size
                terms[:, columns] = (gate * sig * upper).astype(bf16)
                d_up = (d_hidden * gate * sig).astype(bf16)
                d_gate = (d_hidden * upper * sig * (1.0 + gate * (1.0 - sig))).astype(bf16)
                terms[:, place_of(units + first, size)] = d_up
                terms[:, place_of(2 * units + first, size)] = d_gate

            pieces(units, PIECES_B, entry)

            def exit_(columns):
                d_norm = lax.dot_general(
                    terms[:, pl.ds(2 * units, units)], w_gate[columns, :], NT, preferred_element_type=f32
                )
                d_norm = d_norm + lax.dot_general(
                    terms[:, pl.ds(units, units)], w_up[columns, :], NT, preferred_element_type=f32
                )
                wide[:, columns] = d_norm

            xf = x_b[...].astype(f32)
            scale = lax.rsqrt(jnp.mean(xf * xf, axis=-1, keepdims=True) + 1e-06)
            x_hat = xf * scale
            norms[...] = x_hat.astype(bf16)
            if defer:
                return
            pieces(x_b.shape[1], PIECES_B, exit_)
            d_norm = wide[...]
            inner = jnp.mean(d_norm * x_hat, axis=-1, keepdims=True)
            grad = grad_in[...].astype(f32) + scale * (d_norm - x_hat * inner)
            grad = grad.astype(bf16)
            new_grad[...] = grad
            emit("b", pl.ds(0, x_b.shape[1]), grad)


def tick_call(tick, micro, rows, sections, arrays, routes, came, saved):
    _, width = arrays[0].shape
    units = arrays[2].shape[1]
    last = sections - 1
    starts_f, starts_b = starts_of(sections)
    runs_f = 0 <= tick < micro + starts_f[last]
    runs_b = 0 <= tick - starts_b[last] < micro + starts_b[0] - starts_b[last]
    own_f = 0 <= tick < micro
    own_b = 0 <= tick - starts_b[last] < micro
    places = [at for at, _ in saved]
    inputs = (own_f, own_b)
    operands = [a for a, used in zip(arrays, inputs) if used] + list(arrays[2:])
    operands += [value for value, _ in came]
    for _, kept in saved:
        operands += kept
    out_shape = [shape_of(rows, width)] * len(routes)
    if runs_f:
        out_shape += [shape_of(rows, units, dtype=f32)] * 2 + [shape_of(rows, width)]
    if runs_b:
        out_shape += [shape_of(rows, width), shape_of(rows, width), shape_of(rows, 3 * units)]
    loading = tick == 0
    if loading:
        out_shape += [shape_of(*w.shape) for w in arrays[2:]]
    plan = (
        runs_f,
        runs_b,
        routes,
        [takers for _, takers in came],
        places,
        inputs,
        starts_f,
        starts_b,
        loading,
        tick == micro + starts_b[0] - 1,
    )
    result = pl.pallas_call(
        functools.partial(tick_kernel, tick, micro, rows, sections, plan),
        out_shape=out_shape,
        in_specs=[ANY if loading else VM] * len(operands),
        out_specs=[VM] * len(out_shape),
        scratch_shapes=[
            pltpu.VMEM((rows, width), bf16),
            pltpu.VMEM((rows, units), f32),
            pltpu.VMEM((rows, units), f32),
            pltpu.VMEM((rows, width), bf16),
            pltpu.VMEM((rows, width), bf16),
            pltpu.VMEM((rows, units), bf16),
            pltpu.VMEM((rows, width), f32),
        ]
        + [pltpu.SemaphoreType.DMA((4,))] * loading,
        compiler_params=pltpu.CompilerParams(vmem_limit_bytes=(LOAD_MIB if loading else 10) << 20),
        cost_estimate=pl.CostEstimate(
            flops=6 * (runs_f + runs_b) * rows * width * units,
            bytes_accessed=6 * width * units,
            transcendentals=0,
        ),
        name="tick",
    )(*operands)
    result = list(result)
    outs = result[: len(routes)]
    rest = result[len(routes) :]
    loaded = None
    if loading:
        rest, loaded = rest[:-3], rest[-3:]
    kept = rest[:3] if runs_f else None
    terms = rest[-3:] if runs_b else None
    return outs, kept, terms, loaded


def tail_kernel(grad_in, x, terms, w_gate, w_up, after, out, wide):
    units = w_gate.shape[1]

    @pl.when(lax.axis_index("section") == 0)
    def work():
        def exit_(columns):
            d_norm = lax.dot_general(
                terms[:, pl.ds(2 * units, units)], w_gate[columns, :], NT, preferred_element_type=f32
            )
            wide[:, columns] = d_norm + lax.dot_general(
                terms[:, pl.ds(units, units)], w_up[columns, :], NT, preferred_element_type=f32
            )

        pieces(x.shape[1], PIECES_B, exit_)
        xf = x[...].astype(f32)
        scale = lax.rsqrt(jnp.mean(xf * xf, axis=-1, keepdims=True) + 1e-06)
        x_hat = xf * scale
        d_norm = wide[...]
        inner = jnp.mean(d_norm * x_hat, axis=-1, keepdims=True)
        grad = grad_in[...].astype(f32) + scale * (d_norm - x_hat * inner)
        out[...] = grad.astype(bf16)


def tail_call(grad_in, x, terms, w_gate, w_up, after):
    rows, width = x.shape
    units = w_gate.shape[1]
    return pl.pallas_call(
        tail_kernel,
        out_shape=shape_of(rows, width),
        in_specs=[VM] * 5 + [ANY],
        out_specs=VM,
        scratch_shapes=[pltpu.VMEM((rows, width), f32)],
        compiler_params=pltpu.CompilerParams(vmem_limit_bytes=10 << 20),
        cost_estimate=pl.CostEstimate(
            flops=4 * rows * width * units, bytes_accessed=4 * width * units, transcendentals=0
        ),
        name="tail",
    )(grad_in, x, terms, w_gate, w_up, after)


def collect_call(micro, rows, sections, total, whole, sources):
    last = sections - 1
    starts_b = starts_of(sections)[1]
    starts = [min(i * rows, total - rows) for i in range(micro)]
    whole = [] if whole is None else [whole]
    found = []
    at_of = {}
    for tick, value in enumerate(sources):
        by_place = value if isinstance(value, dict) else dict.fromkeys(range(sections), value)
        for at, array in by_place.items():
            known = [i for i, old in enumerate(found) if old is array]
            if not known:
                known = [len(found)]
                found.append(array)
            at_of[tick, at] = known[0]

    def kernel(*refs):
        place = lax.axis_index("section")
        target = refs[-1]
        pool = refs[len(whole) : -1]
        for at in range(sections):

            @pl.when(place == at)
            def take():
                if whole and at == last:
                    target[...] = refs[0][...]
                else:
                    for i, start in enumerate(starts):
                        target[start : start + rows, :] = pool[at_of[i + starts_b[at] - starts_b[last], at]][...]

    operands = whole + found
    width = operands[-1].shape[1]
    return pl.pallas_call(
        kernel,
        out_shape=shape_of(total, width),
        in_specs=[VM] * len(operands),
        out_specs=VM,
        compiler_params=pltpu.CompilerParams(vmem_limit_bytes=10 << 20),
        cost_estimate=pl.CostEstimate(flops=0, bytes_accessed=4 * total * width, transcendentals=0),
        name="collect",
    )(*operands)


def edges_of(sections):
    edges = [("x", at, at + 1) for at in range(sections - 1)]
    return edges + [("b", at, at - 1) for at in range(1, sections)]


def plan_routes(tick, micro, sections):
    starts_f, starts_b = starts_of(sections)
    edges = {}
    for kind, a, b in edges_of(sections):
        start = (starts_b if kind == "b" else starts_f)[a]
        if 0 <= tick - start < micro:
            edges[a, b] = kind
    plans = []
    both = [(a, b) for a, b in edges if a < b and (b, a) in edges]
    for parity in (0, 1):
        chosen = [p for a, b in both if a % 2 == parity for p in ((a, b), (b, a))]
        if chosen:
            plans.append({pair: edges.pop(pair) for pair in chosen})
    for kind in ("x", "b"):
        chosen = [pair for pair, what in edges.items() if what == kind]
        if chosen:
            plans.append({pair: kind for pair in chosen})
    routes = []
    for plan in plans:
        full = dict(plan)
        full = {a: b for a, b in full}
        targets = set(full.values())
        for a in sorted(full):
            if a not in targets:
                end = a
                while end in full:
                    end = full[end]
                full[end] = a
        routes.append((full, [(kind, a, b) for (a, b), kind in plan.items()]))
    return routes


def permute(value, full, sections, lanes):
    pairs = []
    for s in range(sections):
        for d in range(lanes):
            to = full[s] * lanes + d if s in full else s * lanes + (d ^ 1)
            pairs.append((s * lanes + d, to))
    return lax.ppermute(value, ("section", "dp"), pairs)


def weight_kernel(left, right, *refs):
    core = lax.rem(lax.axis_index("dp"), 2)
    keep, send = refs[-2:]
    half = keep.shape[1]
    both = lax.dot_general(left[...], right[...], TN, preferred_element_type=f32).astype(bf16)
    low, high = both[:half], both[half:]

    @pl.when(core == 0)
    def even():
        keep[0] = low
        send[0] = high

    @pl.when(core != 0)
    def odd():
        keep[0] = high
        send[0] = low


def weight_call(chips, left, right, right_at, units, after, ends=False):
    total, width = left.shape
    pair = width // chips
    half = pair // 2
    count = 2 if ends else chips

    def column(i):
        return (0, (chips - 1) * (1 - i) if ends else i)

    return pl.pallas_call(
        weight_kernel,
        out_shape=[shape_of(count, half, units)] * 2,
        grid=(count,),
        in_specs=[
            pl.BlockSpec((total, pair), column),
            pl.BlockSpec((total, units), lambda i: (0, right_at)),
        ]
        + [pl.BlockSpec(memory_space=pl.ANY)] * len(after),
        out_specs=[pl.BlockSpec((1, half, units), lambda i: (i, 0, 0))] * 2,
        compiler_params=pltpu.CompilerParams(vmem_limit_bytes=10 << 20),
        cost_estimate=pl.CostEstimate(
            flops=2 * total * pair * count * units,
            bytes_accessed=4 * pair * count * units,
            transcendentals=0,
        ),
        name="weight",
    )(left, right, *after)


def from_sides(chip, chips, arrived):
    first = arrived[0][...].astype(f32)
    second = arrived[1][...].astype(f32) if len(arrived) > 1 else first
    even = lax.rem(chip, 2) == 0
    left = jnp.where(chip > 0, jnp.where(even, second, first), 0.0)
    right = jnp.where(chip < chips - 1, jnp.where(even, first, second), 0.0)
    return left, right


def step_kernel(step, chips, keep, swapped, *refs):
    chip = lax.div(lax.axis_index("dp"), 2)
    even = lax.rem(chip, 2) == 0
    outs = refs[-2:]
    arrived = refs[:-2]
    if keep.shape[0] < chips:
        to_right, to_left = 0, 1
    else:
        to_right = jnp.clip(chips - step + chip, 0, chips - 1)
        to_left = jnp.clip(step - chips + chip, 0, chips - 1)
    right = keep[to_right].astype(f32) + swapped[to_right].astype(f32)
    left = keep[to_left].astype(f32) + swapped[to_left].astype(f32)
    if arrived:
        from_left, from_right = from_sides(chip, chips, arrived)
        right = right + jnp.where(chip <= step - 1, from_left, 0.0)
        left = left + jnp.where(chip >= chips - step, from_right, 0.0)
    outs[0][...] = jnp.where(even, right, left).astype(bf16)
    outs[1][...] = jnp.where(even, left, right).astype(bf16)


def step_call(step, chips, keep, swapped, arrived):
    half, units = keep.shape[1:]
    return pl.pallas_call(
        functools.partial(step_kernel, step, chips),
        out_shape=[shape_of(half, units)] * 2,
        in_specs=[VM] * (2 + len(arrived)),
        out_specs=[VM, VM],
        compiler_params=pltpu.CompilerParams(vmem_limit_bytes=10 << 20),
        cost_estimate=pl.CostEstimate(flops=half * units, bytes_accessed=half * units, transcendentals=0),
        name="step",
    )(keep, swapped, *arrived)


def final_kernel(chips, keep, swapped, *refs):
    chip = lax.div(lax.axis_index("dp"), 2)
    from_left, from_right = from_sides(chip, chips, refs[:-1])
    refs[-1][...] = keep[chip].astype(f32) + swapped[chip].astype(f32) + from_left + from_right


def final_call(chips, keep, swapped, arrived):
    half, units = keep.shape[1:]
    return pl.pallas_call(
        functools.partial(final_kernel, chips),
        out_shape=shape_of(half, units, dtype=f32),
        in_specs=[VM] * (2 + len(arrived)),
        out_specs=VM,
        compiler_params=pltpu.CompilerParams(vmem_limit_bytes=10 << 20),
        cost_estimate=pl.CostEstimate(flops=half * units, bytes_accessed=half * units, transcendentals=0),
        name="final",
    )(keep, swapped, *arrived)


def body(tokens, cotangent, w_gate, w_up, w_down):
    sections = lax.axis_size("section")
    lanes = lax.axis_size("dp")
    chips = lanes // 2
    total, _ = tokens.shape
    units = w_gate.shape[2]
    rows = ROWS
    micro = -(-total // rows)
    last = sections - 1
    arrays = (tokens, cotangent, w_gate[0], w_up[0], w_down[0])

    starts_f, starts_b = starts_of(sections)
    sent, kept = {}, {}
    arrivals, history = [], []
    for tick in range(micro + starts_b[0]):
        routes = plan_routes(tick, micro, sections)
        came, into = [], {}
        for kind, a, b in edges_of(sections):
            starts = starts_b if kind == "b" else starts_f
            if 0 <= tick - starts[b] < micro:
                value = sent[kind, a, b, tick - starts[b] + starts[a]]
                takers = [old for array, old in came if array is value]
                if not takers:
                    takers = [[]]
                    came.append((value, takers[0]))
                takers[0].append((b, kind))
                if kind == "b":
                    into[b] = value
        saved = []
        for at in range(last):
            index = tick - starts_b[at]
            if 0 <= index < micro:
                saved.append((at, kept[index + starts_f[at]]))
        outs, kept[tick], terms, loaded = tick_call(
            tick,
            micro,
            rows,
            sections,
            arrays,
            [[(a, kind) for kind, a, _ in taken] for _, taken in routes],
            came,
            saved,
        )
        if loaded is not None:
            arrays = (tokens, cotangent, *loaded)
        if terms is not None:
            history.append(terms)
            arrivals.append(into)
        for out, (full, taken) in zip(outs, routes):
            value = permute(out, full, sections, lanes)
            for kind, a, b in taken:
                sent[kind, a, b, tick] = value

    laid = functools.partial(collect_call, micro, rows, sections, total)
    all_in = collect_call(micro, rows, sections, total, arrays[1], arrivals)
    grads, norms, terms = [list(column) for column in zip(*history)]
    last_terms = terms[-1]
    normed, terms = laid(None, norms), laid(None, terms)
    near = [(z, z ^ 1) for z in range(chips)]
    far = [(z, ((z + 1) ^ 1) - 1) for z in range(chips)]
    held = {}

    def begin(which, after):
        left = all_in if which == 0 else normed
        keep, send = weight_call(chips, left, terms, which, units, after)
        held[which] = (keep, permute(send, {}, sections, lanes))

    def advance(step, which, arrived, quick=None):
        keep, swapped = quick or held[which]
        outs = step_call(step, chips, keep, swapped, arrived)
        arrived = [line(outs[0], near, chips)]
        if step > 1 or chips % 2:
            arrived.append(line(outs[1], far, chips))
        return outs[0], arrived

    keep, send = weight_call(chips, all_in, terms, 0, units, [], True)
    quick = (keep, permute(send, {}, sections, lanes))
    begin(1, [send])
    moving = {}
    out, moving[0] = advance(1, 0, [], quick)
    begin(2, [out])
    out, moving[1] = advance(1, 1, [])
    begin(0, [out])
    moving[2] = advance(1, 2, [])[1]
    grads[-1] = tail_call(arrivals[-1][0], kept[micro - 1][2], last_terms, *arrays[2:4], out)
    all_grad = laid(None, grads)
    for step in range(2, chips):
        for which in range(3):
            moving[which] = advance(step, which, moving[which])[1]
    results = [final_call(chips, *held[which], moving[which]) for which in range(3)]
    grad_d, grad_u, grad_g = results
    return (all_grad[None], grad_g[None], grad_u[None], grad_d[None])


def line(value, pairs, chips):
    route = []
    for z, to in pairs:
        for c in range(2):
            route.append((2 * z + c, 2 * to + c if 0 <= to < chips else 2 * z + 1 - c))
    return lax.ppermute(value, "dp", route)


def solution(mesh):
    placed = (
        P("dp", None),
        P("dp", None),
        P("section", None, None),
        P("section", None, None),
        P("section", None, None),
    )
    return jax.shard_map(
        body,
        mesh=mesh,
        in_specs=placed,
        out_specs=(
            P("section", "dp", None),
            P("section", "dp", None),
            P("section", "dp", None),
            P("section", "dp", None),
        ),
        check_vma=False,
    )
```

```python
import functools

import jax
import jax.numpy as jnp
from jax import lax
from jax.experimental import pallas as pl
from jax.experimental.pallas import tpu as pltpu
from jax.sharding import PartitionSpec as P


ROWS = 48
LAGS_F = (2, 2, 2)
LAGS_B = (2, 2, 2)
LOAD_MIB = 44
PIECES_F = 2
PIECES_B = 2


f32 = jnp.float32
bf16 = jnp.bfloat16
NT = (((1,), (1,)), ((), ()))
TN = (((0,), (0,)), ((), ()))
VM = pl.BlockSpec(memory_space=pltpu.VMEM)
ANY = pl.BlockSpec(memory_space=pl.ANY)


def shape_of(*dims, dtype=bf16):
    return jax.ShapeDtypeStruct(dims, dtype)


def pieces(size, count, body):
    step = size // count
    if count == 1:
        body(pl.ds(0, size))
        return

    def one(i, carry):
        body(pl.ds(pl.multiple_of(i * step, step), step))
        return carry

    lax.fori_loop(0, count, one, 0)


def place_of(start, size):
    return pl.ds(start if isinstance(start, int) else pl.multiple_of(start, size), size)


def pick_of(place, values):
    result = values[0]
    for at, value in enumerate(values[1:]):
        result = jnp.where(place > at, value, result)
    return result


def lag_of(lags, hop):
    return lags[hop] if hop < len(lags) else lags[-1]


def starts_of(sections):
    last = sections - 1
    forward = [0]
    for hop in range(last):
        forward.append(forward[-1] + lag_of(LAGS_F, hop))
    backward = [forward[-1]]
    for hop in range(last):
        backward.append(backward[-1] + lag_of(LAGS_B, hop))
    return forward, backward[::-1]


def tick_kernel(tick, micro, rows, sections, plan, *refs):
    runs_f, runs_b, routes, arrivals, places, inputs, starts_f, starts_b, loading, defer = plan
    refs = list(refs)
    place = lax.axis_index("section")
    tokens = refs.pop(0) if inputs[0] else None
    cotangent = refs.pop(0) if inputs[1] else None
    w_gate, w_up, w_down = refs[:3]
    refs = refs[3:]
    loads = []
    if loading:
        sems = refs.pop()
        sources = [tokens.at[pl.ds(0, rows), :], w_gate, w_up, w_down]
    arrived = [(refs.pop(0), takers) for takers in arrivals]
    saved = []
    for at in places:
        saved.append((at, refs[:3]))
        refs = refs[3:]
    outs = [refs.pop(0) for _ in routes]
    if runs_f:
        gate_f, up_f, x_f, hidden = refs[:4]
        refs = refs[4:]
    if runs_b:
        new_grad, norms, terms = refs[:3]
        refs = refs[3:]
    if loading:
        w_gate, w_up, w_down = refs[:3]
        refs = refs[3:]
        targets = [x_f, w_gate, w_up, w_down]
        for number in range(4):
            copy = pltpu.make_async_copy(sources[number], targets[number], sems.at[number])
            copy.start()
            loads.append(copy)
    x_b, gate_b, up_b, grad_in, normed, wide = refs
    last = sections - 1
    units = w_gate.shape[1]
    index_f = tick - pick_of(place, starts_f)
    index_b = tick - pick_of(place, starts_b)

    def window(index, source):
        total = source.shape[0]
        start = jnp.clip(index * rows, 0, total - rows)
        return source[pl.ds(pl.multiple_of(start, 16), rows), :]

    good_f = (index_f >= 0) & (index_f < micro)
    good_b = (index_b >= 0) & (index_b < micro)

    def emit(kind, columns, value):
        for out, route in zip(outs, routes):
            senders = [s for s, what in route if what == kind]
            if senders:
                hit = functools.reduce(jnp.logical_or, [place == s for s in senders])

                @pl.when(hit)
                def send():
                    out[:, columns] = value

    def receive(kind, target, source, owner, index):
        if source is not None:

            @pl.when(place == owner)
            def own():
                target[...] = window(index, source)

        for value, takers in arrived:
            for s, what in takers:
                if what == kind:

                    @pl.when(place == s)
                    def passed():
                        target[...] = value[...]

    if runs_f:

        @pl.when(good_f)
        def forward():
            if loading:
                loads[0].wait()
            else:
                receive("x", x_f, tokens, 0, index_f)
            xf = x_f[...].astype(f32)
            scale = lax.rsqrt(jnp.mean(xf * xf, axis=-1, keepdims=True) + 1e-06)
            normed[...] = (xf * scale).astype(bf16)

            def entry(columns):
                value = normed[...]
                gate = jnp.dot(value, w_gate[:, columns], preferred_element_type=f32)
                upper = jnp.dot(value, w_up[:, columns], preferred_element_type=f32)
                gate_f[:, columns] = gate
                up_f[:, columns] = upper
                value = (gate * jax.nn.sigmoid(gate) * upper).astype(bf16)
                hidden[:, columns] = value

            for copy in loads[1:3]:
                copy.wait()
            pieces(units, PIECES_F, entry)
            for copy in loads[3:]:
                copy.wait()

            @pl.when(place != last)
            def exit_():
                def down(columns):
                    branch = lax.dot_general(
                        hidden[...], w_down[columns, :], NT, preferred_element_type=f32
                    )
                    value = (x_f[:, columns].astype(f32) + branch).astype(bf16)
                    emit("x", columns, value)

                pieces(x_f.shape[1], PIECES_F, down)

    if loading:

        @pl.when(jnp.logical_not(good_f))
        def idle():
            for copy in loads:
                copy.wait()

    if runs_b:

        @pl.when(good_b)
        def backward():
            receive("b", grad_in, cotangent, last, index_b)
            for at, kept in saved:

                @pl.when(place == at)
                def take():
                    gate_b[...] = kept[0][...]
                    up_b[...] = kept[1][...]
                    x_b[...] = kept[2][...]

            if runs_f:

                @pl.when(place == last)
                def same():
                    gate_b[...] = gate_f[...]
                    up_b[...] = up_f[...]
                    x_b[...] = x_f[...]

            def entry(columns):
                d_hidden = jnp.dot(grad_in[...], w_down[:, columns], preferred_element_type=f32)
                gate = gate_b[:, columns]
                upper = up_b[:, columns]
                sig = jax.nn.sigmoid(gate)
                first = columns.start
                size = columns.size
                terms[:, columns] = (gate * sig * upper).astype(bf16)
                d_up = (d_hidden * gate * sig).astype(bf16)
                d_gate = (d_hidden * upper * sig * (1.0 + gate * (1.0 - sig))).astype(bf16)
                terms[:, place_of(units + first, size)] = d_up
                terms[:, place_of(2 * units + first, size)] = d_gate

            pieces(units, PIECES_B, entry)

            def exit_(columns):
                d_norm = lax.dot_general(
                    terms[:, pl.ds(2 * units, units)], w_gate[columns, :], NT, preferred_element_type=f32
                )
                d_norm = d_norm + lax.dot_general(
                    terms[:, pl.ds(units, units)], w_up[columns, :], NT, preferred_element_type=f32
                )
                wide[:, columns] = d_norm

            xf = x_b[...].astype(f32)
            scale = lax.rsqrt(jnp.mean(xf * xf, axis=-1, keepdims=True) + 1e-06)
            x_hat = xf * scale
            norms[...] = x_hat.astype(bf16)
            if defer:
                return
            pieces(x_b.shape[1], PIECES_B, exit_)
            d_norm = wide[...]
            inner = jnp.mean(d_norm * x_hat, axis=-1, keepdims=True)
            grad = grad_in[...].astype(f32) + scale * (d_norm - x_hat * inner)
            grad = grad.astype(bf16)
            new_grad[...] = grad
            emit("b", pl.ds(0, x_b.shape[1]), grad)


def tick_call(tick, micro, rows, sections, arrays, routes, came, saved):
    _, width = arrays[0].shape
    units = arrays[2].shape[1]
    last = sections - 1
    starts_f, starts_b = starts_of(sections)
    runs_f = 0 <= tick < micro + starts_f[last]
    runs_b = 0 <= tick - starts_b[last] < micro + starts_b[0] - starts_b[last]
    own_f = 0 <= tick < micro
    own_b = 0 <= tick - starts_b[last] < micro
    places = [at for at, _ in saved]
    inputs = (own_f, own_b)
    operands = [a for a, used in zip(arrays, inputs) if used] + list(arrays[2:])
    operands += [value for value, _ in came]
    for _, kept in saved:
        operands += kept
    out_shape = [shape_of(rows, width)] * len(routes)
    if runs_f:
        out_shape += [shape_of(rows, units, dtype=f32)] * 2 + [shape_of(rows, width), shape_of(rows, units)]
    if runs_b:
        out_shape += [shape_of(rows, width), shape_of(rows, width), shape_of(rows, 3 * units)]
    loading = tick == 0
    if loading:
        out_shape += [shape_of(*w.shape) for w in arrays[2:]]
    plan = (
        runs_f,
        runs_b,
        routes,
        [takers for _, takers in came],
        places,
        inputs,
        starts_f,
        starts_b,
        loading,
        tick == micro + starts_b[0] - 1,
    )
    result = pl.pallas_call(
        functools.partial(tick_kernel, tick, micro, rows, sections, plan),
        out_shape=out_shape,
        in_specs=[ANY if loading else VM] * len(operands),
        out_specs=[VM] * len(out_shape),
        scratch_shapes=[
            pltpu.VMEM((rows, width), bf16),
            pltpu.VMEM((rows, units), f32),
            pltpu.VMEM((rows, units), f32),
            pltpu.VMEM((rows, width), bf16),
            pltpu.VMEM((rows, width), bf16),
            pltpu.VMEM((rows, width), f32),
        ]
        + [pltpu.SemaphoreType.DMA((4,))] * loading,
        compiler_params=pltpu.CompilerParams(vmem_limit_bytes=(LOAD_MIB if loading else 10) << 20),
        cost_estimate=pl.CostEstimate(
            flops=6 * (runs_f + runs_b) * rows * width * units,
            bytes_accessed=6 * width * units,
            transcendentals=0,
        ),
        name="tick",
    )(*operands)
    result = list(result)
    outs = result[: len(routes)]
    rest = result[len(routes) :]
    loaded = None
    if loading:
        rest, loaded = rest[:-3], rest[-3:]
    kept = rest[:4] if runs_f else None
    terms = rest[-3:] if runs_b else None
    return outs, kept, terms, loaded


def tail_kernel(grad_in, x, terms, w_gate, w_up, after, out, wide):
    units = w_gate.shape[1]

    @pl.when(lax.axis_index("section") == 0)
    def work():
        def exit_(columns):
            d_norm = lax.dot_general(
                terms[:, pl.ds(2 * units, units)], w_gate[columns, :], NT, preferred_element_type=f32
            )
            wide[:, columns] = d_norm + lax.dot_general(
                terms[:, pl.ds(units, units)], w_up[columns, :], NT, preferred_element_type=f32
            )

        pieces(x.shape[1], PIECES_B, exit_)
        xf = x[...].astype(f32)
        scale = lax.rsqrt(jnp.mean(xf * xf, axis=-1, keepdims=True) + 1e-06)
        x_hat = xf * scale
        d_norm = wide[...]
        inner = jnp.mean(d_norm * x_hat, axis=-1, keepdims=True)
        grad = grad_in[...].astype(f32) + scale * (d_norm - x_hat * inner)
        out[...] = grad.astype(bf16)


def tail_call(grad_in, x, terms, w_gate, w_up, after):
    rows, width = x.shape
    units = w_gate.shape[1]
    return pl.pallas_call(
        tail_kernel,
        out_shape=shape_of(rows, width),
        in_specs=[VM] * 5 + [ANY],
        out_specs=VM,
        scratch_shapes=[pltpu.VMEM((rows, width), f32)],
        compiler_params=pltpu.CompilerParams(vmem_limit_bytes=10 << 20),
        cost_estimate=pl.CostEstimate(
            flops=4 * rows * width * units, bytes_accessed=4 * width * units, transcendentals=0
        ),
        name="tail",
    )(grad_in, x, terms, w_gate, w_up, after)


def collect_call(micro, rows, sections, total, whole, sources, forward=False):
    last = sections - 1
    first = starts_of(sections)[0 if forward else 1]
    base = min(first)
    starts = [min(i * rows, total - rows) for i in range(micro)]
    whole = [] if whole is None else [whole]
    found = []
    at_of = {}
    for tick, value in enumerate(sources):
        by_place = value if isinstance(value, dict) else dict.fromkeys(range(sections), value)
        for at, array in by_place.items():
            known = [i for i, old in enumerate(found) if old is array]
            if not known:
                known = [len(found)]
                found.append(array)
            at_of[tick, at] = known[0]

    def kernel(*refs):
        place = lax.axis_index("section")
        target = refs[-1]
        pool = refs[len(whole) : -1]
        for at in range(sections):

            @pl.when(place == at)
            def take():
                if whole and at == last:
                    target[...] = refs[0][...]
                else:
                    for i, start in enumerate(starts):
                        target[start : start + rows, :] = pool[at_of[i + first[at] - base, at]][...]

    operands = whole + found
    width = operands[-1].shape[1]
    return pl.pallas_call(
        kernel,
        out_shape=shape_of(total, width),
        in_specs=[VM] * len(operands),
        out_specs=VM,
        compiler_params=pltpu.CompilerParams(vmem_limit_bytes=10 << 20),
        cost_estimate=pl.CostEstimate(flops=0, bytes_accessed=4 * total * width, transcendentals=0),
        name="collect",
    )(*operands)


def edges_of(sections):
    edges = [("x", at, at + 1) for at in range(sections - 1)]
    return edges + [("b", at, at - 1) for at in range(1, sections)]


def plan_routes(tick, micro, sections):
    starts_f, starts_b = starts_of(sections)
    edges = {}
    for kind, a, b in edges_of(sections):
        start = (starts_b if kind == "b" else starts_f)[a]
        if 0 <= tick - start < micro:
            edges[a, b] = kind
    plans = []
    both = [(a, b) for a, b in edges if a < b and (b, a) in edges]
    for parity in (0, 1):
        chosen = [p for a, b in both if a % 2 == parity for p in ((a, b), (b, a))]
        if chosen:
            plans.append({pair: edges.pop(pair) for pair in chosen})
    for kind in ("x", "b"):
        chosen = [pair for pair, what in edges.items() if what == kind]
        if chosen:
            plans.append({pair: kind for pair in chosen})
    routes = []
    for plan in plans:
        full = dict(plan)
        full = {a: b for a, b in full}
        targets = set(full.values())
        for a in sorted(full):
            if a not in targets:
                end = a
                while end in full:
                    end = full[end]
                full[end] = a
        routes.append((full, [(kind, a, b) for (a, b), kind in plan.items()]))
    return routes


def permute(value, full, sections, lanes):
    pairs = []
    for s in range(sections):
        for d in range(lanes):
            to = full[s] * lanes + d if s in full else s * lanes + (d ^ 1)
            pairs.append((s * lanes + d, to))
    return lax.ppermute(value, ("section", "dp"), pairs)


def weight_kernel(left, right, *refs):
    core = lax.rem(lax.axis_index("dp"), 2)
    keep, send = refs[-2:]
    half = keep.shape[1]
    both = lax.dot_general(left[...], right[...], TN, preferred_element_type=f32).astype(bf16)
    low, high = both[:half], both[half:]

    @pl.when(core == 0)
    def even():
        keep[0] = low
        send[0] = high

    @pl.when(core != 0)
    def odd():
        keep[0] = high
        send[0] = low


def weight_call(chips, left, right, right_at, units, after, ends=False):
    total, width = left.shape
    pair = width // chips
    half = pair // 2
    count = 2 if ends else chips

    def column(i):
        return (0, (chips - 1) * (1 - i) if ends else i)

    return pl.pallas_call(
        weight_kernel,
        out_shape=[shape_of(count, half, units)] * 2,
        grid=(count,),
        in_specs=[
            pl.BlockSpec((total, pair), column),
            pl.BlockSpec((total, units), lambda i: (0, right_at)),
        ]
        + [pl.BlockSpec(memory_space=pl.ANY)] * len(after),
        out_specs=[pl.BlockSpec((1, half, units), lambda i: (i, 0, 0))] * 2,
        compiler_params=pltpu.CompilerParams(vmem_limit_bytes=10 << 20),
        cost_estimate=pl.CostEstimate(
            flops=2 * total * pair * count * units,
            bytes_accessed=4 * pair * count * units,
            transcendentals=0,
        ),
        name="weight",
    )(left, right, *after)


def from_sides(chip, chips, arrived):
    first = arrived[0][...].astype(f32)
    second = arrived[1][...].astype(f32) if len(arrived) > 1 else first
    even = lax.rem(chip, 2) == 0
    left = jnp.where(chip > 0, jnp.where(even, second, first), 0.0)
    right = jnp.where(chip < chips - 1, jnp.where(even, first, second), 0.0)
    return left, right


def step_kernel(step, chips, keep, swapped, *refs):
    chip = lax.div(lax.axis_index("dp"), 2)
    even = lax.rem(chip, 2) == 0
    outs = refs[-2:]
    arrived = refs[:-2]
    if keep.shape[0] < chips:
        to_right, to_left = 0, 1
    else:
        to_right = jnp.clip(chips - step + chip, 0, chips - 1)
        to_left = jnp.clip(step - chips + chip, 0, chips - 1)
    right = keep[to_right].astype(f32) + swapped[to_right].astype(f32)
    left = keep[to_left].astype(f32) + swapped[to_left].astype(f32)
    if arrived:
        from_left, from_right = from_sides(chip, chips, arrived)
        right = right + jnp.where(chip <= step - 1, from_left, 0.0)
        left = left + jnp.where(chip >= chips - step, from_right, 0.0)
    outs[0][...] = jnp.where(even, right, left).astype(bf16)
    outs[1][...] = jnp.where(even, left, right).astype(bf16)


def step_call(step, chips, keep, swapped, arrived):
    half, units = keep.shape[1:]
    return pl.pallas_call(
        functools.partial(step_kernel, step, chips),
        out_shape=[shape_of(half, units)] * 2,
        in_specs=[VM] * (2 + len(arrived)),
        out_specs=[VM, VM],
        compiler_params=pltpu.CompilerParams(vmem_limit_bytes=10 << 20),
        cost_estimate=pl.CostEstimate(flops=half * units, bytes_accessed=half * units, transcendentals=0),
        name="step",
    )(keep, swapped, *arrived)


def final_kernel(chips, keep, swapped, *refs):
    chip = lax.div(lax.axis_index("dp"), 2)
    from_left, from_right = from_sides(chip, chips, refs[:-1])
    refs[-1][...] = keep[chip].astype(f32) + swapped[chip].astype(f32) + from_left + from_right


def final_call(chips, keep, swapped, arrived):
    half, units = keep.shape[1:]
    return pl.pallas_call(
        functools.partial(final_kernel, chips),
        out_shape=shape_of(half, units, dtype=f32),
        in_specs=[VM] * (2 + len(arrived)),
        out_specs=VM,
        compiler_params=pltpu.CompilerParams(vmem_limit_bytes=10 << 20),
        cost_estimate=pl.CostEstimate(flops=half * units, bytes_accessed=half * units, transcendentals=0),
        name="final",
    )(keep, swapped, *arrived)


def body(tokens, cotangent, w_gate, w_up, w_down):
    sections = lax.axis_size("section")
    lanes = lax.axis_size("dp")
    chips = lanes // 2
    total, _ = tokens.shape
    units = w_gate.shape[2]
    rows = ROWS
    micro = -(-total // rows)
    last = sections - 1
    arrays = (tokens, cotangent, w_gate[0], w_up[0], w_down[0])

    starts_f, starts_b = starts_of(sections)
    sent, kept = {}, {}
    arrivals, history = [], []
    for tick in range(micro + starts_b[0]):
        routes = plan_routes(tick, micro, sections)
        came, into = [], {}
        for kind, a, b in edges_of(sections):
            starts = starts_b if kind == "b" else starts_f
            if 0 <= tick - starts[b] < micro:
                value = sent[kind, a, b, tick - starts[b] + starts[a]]
                takers = [old for array, old in came if array is value]
                if not takers:
                    takers = [[]]
                    came.append((value, takers[0]))
                takers[0].append((b, kind))
                if kind == "b":
                    into[b] = value
        saved = []
        for at in range(last):
            index = tick - starts_b[at]
            if 0 <= index < micro:
                saved.append((at, kept[index + starts_f[at]][:3]))
        outs, kept[tick], terms, loaded = tick_call(
            tick,
            micro,
            rows,
            sections,
            arrays,
            [[(a, kind) for kind, a, _ in taken] for _, taken in routes],
            came,
            saved,
        )
        if loaded is not None:
            arrays = (tokens, cotangent, *loaded)
        if terms is not None:
            history.append(terms)
            arrivals.append(into)
        for out, (full, taken) in zip(outs, routes):
            value = permute(out, full, sections, lanes)
            for kind, a, b in taken:
                sent[kind, a, b, tick] = value

    laid = functools.partial(collect_call, micro, rows, sections, total)
    all_in = collect_call(micro, rows, sections, total, arrays[1], arrivals)
    grads, norms, terms = [list(column) for column in zip(*history)]
    last_terms = terms[-1]
    hiddens = [kept[n][3] for n in range(micro + starts_f[last])]
    hiddens = collect_call(micro, rows, sections, total, None, hiddens, True)
    normed, terms = laid(None, norms), laid(None, terms)
    near = [(z, z ^ 1) for z in range(chips)]
    far = [(z, ((z + 1) ^ 1) - 1) for z in range(chips)]
    held = {}

    def begin(which, after):
        left = all_in if which == 0 else normed
        keep, send = weight_call(chips, left, terms, which, units, after)
        held[which] = (keep, permute(send, {}, sections, lanes))

    def advance(step, which, arrived, quick=None):
        keep, swapped = quick or held[which]
        outs = step_call(step, chips, keep, swapped, arrived)
        arrived = [line(outs[0], near, chips)]
        if step > 1 or chips % 2:
            arrived.append(line(outs[1], far, chips))
        return outs[0], arrived

    keep, send = weight_call(chips, all_in, hiddens, 0, units, [], True)
    quick = (keep, permute(send, {}, sections, lanes))
    moving = {}
    out, moving[0] = advance(1, 0, [], quick)
    begin(1, [out])
    begin(2, [out])
    out, moving[1] = advance(1, 1, [])
    begin(0, [out])
    moving[2] = advance(1, 2, [])[1]
    grads[-1] = tail_call(arrivals[-1][0], kept[micro - 1][2], last_terms, *arrays[2:4], out)
    all_grad = laid(None, grads)
    for step in range(2, chips):
        for which in range(3):
            moving[which] = advance(step, which, moving[which])[1]
    results = [final_call(chips, *held[which], moving[which]) for which in range(3)]
    grad_d, grad_u, grad_g = results
    return (all_grad[None], grad_g[None], grad_u[None], grad_d[None])


def line(value, pairs, chips):
    route = []
    for z, to in pairs:
        for c in range(2):
            route.append((2 * z + c, 2 * to + c if 0 <= to < chips else 2 * z + 1 - c))
    return lax.ppermute(value, "dp", route)


def solution(mesh):
    placed = (
        P("dp", None),
        P("dp", None),
        P("section", None, None),
        P("section", None, None),
        P("section", None, None),
    )
    return jax.shard_map(
        body,
        mesh=mesh,
        in_specs=placed,
        out_specs=(
            P("section", "dp", None),
            P("section", "dp", None),
            P("section", "dp", None),
            P("section", "dp", None),
        ),
        check_vma=False,
    )
```
